128 devices in a mesh: gx: 16 (over z, y_lo, core), gy: 8 (over x, y_hi).
Axes of the slice: x: 4, y: 4 (y_hi: 2, y_lo: 2; y = y_hi * 2 + y_lo), z: 4, core: 2. Of those that a mesh axis runs over, the one named last changes fastest.
Arguments:
- mean_field: float32 [256, 512, 128], P('gx', 'gy'), may hold values from -3 to 3
- log_scale: float32 [256, 512, 128], P('gx', 'gy'), may hold values from -2.5 to -0.7
- noise: float32 [256, 512, 128], P('gx', 'gy'), may hold values from -6 to 6
- wave_prev: float32 [256, 512, 128], P('gx', 'gy'), may hold values from -6 to 6
- wave_now: float32 [256, 512, 128], P('gx', 'gy'), may hold values from -6 to 6
- adjoint_next: float32 [256, 512, 128], P('gx', 'gy'), may hold values from -6 to 6
- adjoint_now: float32 [256, 512, 128], P('gx', 'gy'), may hold values from -6 to 6
- sources: int32 [16, 3], replicated, may hold values from 0 to 511, as said below
- receivers: int32 [256, 3], replicated, may hold values from 0 to 511, as said below
- observed: float32 [256], replicated, may hold values from -6 to 6
- step_index: int32 [1], replicated, may hold values from 0 to 47
- prior_scale: float32 [1], replicated, may hold values from 0.5 to 2
Outputs:
- wave_next: float32 [256, 512, 128], P('gx', 'gy')
- adjoint_prev: float32 [256, 512, 128], P('gx', 'gy')
- search: float32 [256, 512, 128], P('gx', 'gy')
- logscale_grad: float32 [256, 512, 128], P('gx', 'gy')
The draws below stay inside these ranges and needn't reach their ends.
Inputs may be any that keep to these rules, and one draw needn't show every extreme that they name: `sources`: each row gives the first, second and depth cell of a point, below 256, 512 and 128; points may coincide. `receivers`: each row gives the first, second and depth cell of a point, below 256, 512 and 128; points may coincide.
All inputs are finite; a program needn't handle non-finite values.
Results may differ from the reference program's by a relative error of at most 0.000075.
Values sent between devices are 32-bit elements; how exact they have to be, the bound alone decides.
No kernel may reach another device: no remote copies, remote signals or barrier semaphores. Data moves between devices by JAX's collectives and lax.ppermute only.
A program may use at most 64 MiB of HBM per device.

```python
import math
import jax
import jax.numpy as jnp
from jax import lax

NZ = 128
NSRC = 16
NREC = 256
NSTEPS = 48
NX = 256
NY = 512


def scatter_points(key, number):
    pieces = jax.random.split(key, 3)
    across = jax.random.randint(pieces[0], (number,), 0, NX)
    lateral = jax.random.randint(pieces[1], (number,), 0, NY)
    levels = jax.random.randint(pieces[2], (number,), 0, NZ)
    ordinal = lax.iota(jnp.int32, number)
    across = jnp.where(ordinal == 0, NX - 1, across)
    lateral = jnp.where(ordinal == 1, NY - 1, lateral)
    levels = jnp.where(ordinal == 0, 0, levels)
    levels = jnp.where(ordinal == 1, NZ - 1, levels)
    return jnp.stack([across, lateral, levels], axis=1).astype(jnp.int32)


def draw_sources(key, part):
    return scatter_points(jax.random.fold_in(key, 11), NSRC)


def draw_receivers(key, part):
    return scatter_points(jax.random.fold_in(key, 23), NREC)


def block_scale(stream_key, extent, cuts, low, largest):
    loudness = 1.0
    for axis_at, shards_of in cuts:
        draws = jax.random.uniform(jax.random.fold_in(jax.random.fold_in(stream_key, 6), axis_at), (shards_of,), jnp.float32, low / len(cuts), largest / len(cuts))
        loudness = loudness * jnp.repeat(jnp.exp(draws), extent[axis_at] // shards_of).reshape((-1,) + (1,) * (len(extent) - 1 - axis_at))
    return loudness


def centred(rng, shape, scale, bound, cuts=(), held_as=jnp.bfloat16):
    loudness = block_scale(rng, shape, cuts, -0.22, 0.18) if cuts else 1.0
    array = jax.random.normal(rng, shape, jnp.float32) * scale * loudness
    return jnp.minimum(jnp.maximum(array, -bound), bound).astype(held_as)


def setup_inputs(seed: int = 0) -> dict:
    arg_keys = jax.random.split(jax.random.key(seed), 13)
    mean_field = centred(arg_keys[0], (NX, NY, NZ), 0.5, 3.0, ((0, 16), (1, 8)), jnp.float32)
    log_scale = jnp.clip(-2.5 + 1.8 * jax.random.uniform(arg_keys[1], (NX, NY, NZ), jnp.float32) ** block_scale(arg_keys[1], (NX, NY, NZ), ((0, 16), (1, 8)), -0.2, 0.2), -2.5, -0.7)
    noise = centred(arg_keys[2], (NX, NY, NZ), 1.0, 6.0, ((0, 16), (1, 8)), jnp.float32)
    wave_prev = centred(arg_keys[3], (NX, NY, NZ), 1.0, 6.0, ((0, 16), (1, 8)), jnp.float32)
    wave_now = centred(arg_keys[4], (NX, NY, NZ), 1.0, 6.0, ((0, 16), (1, 8)), jnp.float32)
    adjoint_next = centred(arg_keys[5], (NX, NY, NZ), 1.0, 6.0, ((0, 16), (1, 8)), jnp.float32)
    adjoint_now = centred(arg_keys[6], (NX, NY, NZ), 1.0, 6.0, ((0, 16), (1, 8)), jnp.float32)
    sources = draw_sources(jax.random.fold_in(arg_keys[12], 71), 0)
    receivers = draw_receivers(jax.random.fold_in(arg_keys[12], 71), 0)
    observed = centred(arg_keys[9], (NREC,), 1.0, 6.0, (), jnp.float32)
    step_index = jax.random.randint(arg_keys[10], (1,), 0, NSTEPS).astype(jnp.int32)
    prior_scale = jnp.clip(jnp.exp(jax.random.uniform(arg_keys[11], (1,), jnp.float32, math.log(0.5), math.log(2.0))), 0.5, 2.0)
    return dict(mean_field=mean_field, log_scale=log_scale, noise=noise, wave_prev=wave_prev, wave_now=wave_now, adjoint_next=adjoint_next, adjoint_now=adjoint_now, sources=sources, receivers=receivers, observed=observed, step_index=step_index, prior_scale=prior_scale)


STENCIL_WEIGHTS = (-205.0 / 72.0, 8.0 / 5.0, -1.0 / 5.0, 8.0 / 315.0, -1.0 / 560.0)
COURANT_SQUARED = 0.08
VELOCITY_GAIN = 0.2
PULSE_FREQUENCY = 0.05
PULSE_AMPLITUDE = 20.0

def shifted(padded, dimension, offset):
    result = padded
    for axis_number in range(3):
        anchor = 4 + offset if axis_number == dimension else 4
        length = padded.shape[axis_number] - 8
        result = lax.slice_in_dim(result, anchor, anchor + length, axis=axis_number)
    return result

def laplacian(field):
    padded = jnp.pad(field, 4)
    summed = 3.0 * STENCIL_WEIGHTS[0] * field
    for offset in range(1, 5):
        for dimension in range(3):
            summed = summed + STENCIL_WEIGHTS[offset] * (shifted(padded, dimension, offset) + shifted(padded, dimension, -offset))
    return summed

def inject(field, points, values):
    return field.at[points[:, 0], points[:, 1], points[:, 2]].add(values)

def wave_term(count, length):
    waves = jnp.arange(count, dtype=jnp.int32).astype(jnp.float32)
    sine = jnp.sin(waves * (math.pi / length))
    return (length / 8.0) ** 2 * 4.0 * sine * sine

def reference(mean_field, log_scale, noise, wave_prev, wave_now, adjoint_next, adjoint_now, sources, receivers, observed, step_index, prior_scale):
    spread = jnp.exp(log_scale)
    sample = mean_field + spread * noise
    speed = COURANT_SQUARED * jnp.exp(2.0 * VELOCITY_GAIN * sample)
    moment = (step_index[0] - NSTEPS // 2).astype(jnp.float32) * (math.pi * PULSE_FREQUENCY)
    pulse = PULSE_AMPLITUDE * (1.0 - 2.0 * moment * moment) * jnp.exp(-moment * moment)
    curved = laplacian(wave_now)
    wave_next = 2.0 * wave_now - wave_prev + speed * curved
    wave_next = inject(wave_next, sources, jnp.ones((NSRC,), jnp.float32) * pulse)
    misfit = wave_next[receivers[:, 0], receivers[:, 1], receivers[:, 2]] - observed
    adjoint_prev = 2.0 * adjoint_now - adjoint_next + laplacian(speed * adjoint_now)
    adjoint_prev = inject(adjoint_prev, receivers, misfit)
    data_grad = 2.0 * VELOCITY_GAIN * speed * adjoint_prev * curved
    half_depth = NZ // 2 + 1
    denominator = 1.0 + wave_term(NX, NX)[:, None, None] + wave_term(NY, NY)[None, :, None] + wave_term(half_depth, NZ)[None, None, :]
    gain = prior_scale[0] * (math.sqrt(NX * NY * NZ) / 8.0) / denominator
    spectrum = jnp.fft.rfftn(data_grad)
    smooth = jnp.fft.irfftn(spectrum * gain, s=(NX, NY, NZ))
    search = smooth.astype(jnp.float32) + sample
    logscale_grad = data_grad * spread * noise - 1.0
    return (wave_next, adjoint_prev, search, logscale_grad)
```

```python
import functools
import math

import jax
import jax.numpy as jnp
import numpy as np
from jax import lax
from jax.experimental import pallas as pl
from jax.experimental.pallas import tpu as pltpu
from jax.sharding import PartitionSpec as P

NSTEPS = 48
STENCIL_WEIGHTS = (-205.0 / 72.0, 8.0 / 5.0, -1.0 / 5.0, 8.0 / 315.0, -1.0 / 560.0)
COURANT_SQUARED = 0.08
VELOCITY_GAIN = 0.2
PULSE_FREQUENCY = 0.05
PULSE_AMPLITUDE = 20.0

F32 = jnp.float32
BF16 = jnp.bfloat16
ROW = (((1,), (0,)), ((), ()))
TRANSPOSED_RIGHT = (((1,), (1,)), ((), ()))
TRANSPOSED_LEFT = (((0,), (0,)), ((), ()))


def hartley(length):
    index = np.arange(length)
    angle = (index[:, None] * index[None, :] % length) * (2.0 * np.pi / length)
    return np.cos(angle) + np.sin(angle)


def halves(matrix):
    high = matrix.astype(np.float32).astype(jnp.bfloat16)
    low = (matrix - high.astype(np.float64)).astype(np.float32).astype(jnp.bfloat16)
    return np.stack([high, low])


def wave_terms(length):
    return (length / 8.0) ** 2 * 4.0 * np.sin(np.arange(length) * (np.pi / length)) ** 2


def band(length):
    matrix = np.zeros((length, length))
    for offset in range(5):
        weight = STENCIL_WEIGHTS[offset] * (3.0 if offset == 0 else 1.0)
        matrix += weight * np.eye(length, k=offset)
        if offset:
            matrix += weight * np.eye(length, k=-offset)
    return matrix


def split(value):
    high = value.astype(BF16)
    return high, (value - high.astype(F32)).astype(BF16)


def dot(left, right, dims=ROW):
    return lax.dot_general(left, right, dims, preferred_element_type=F32)


def dot_3(left, right, dims=ROW):
    total = dot(left[0], right[1], dims) + dot(left[1], right[0], dims)
    return total + dot(left[0], right[0], dims)


def edges_kernel(mean, logs, noise, adjoint, wave, xlow, xhigh, ylow, yhigh):
    nx, ny, _ = wave.shape

    def scaled(a, b, c, d):
        where = (slice(a, b), slice(c, d))
        sample = mean[where] + jnp.exp(logs[where]) * noise[where]
        return COURANT_SQUARED * jnp.exp(2.0 * VELOCITY_GAIN * sample) * adjoint[where]

    xlow[0] = wave[0:4]
    xhigh[0] = wave[nx - 4 : nx]
    xlow[1] = scaled(0, 4, 0, ny)
    xhigh[1] = scaled(nx - 4, nx, 0, ny)
    for start in range(0, nx, 4):
        if start == 0:
            low, high = xlow[1, :, 0:8], xhigh[1, :, 0:8]
        for kind in range(2):
            if kind == 0:
                first, last = wave[start : start + 4, 0:8], wave[start : start + 4, ny - 8 : ny]
            elif start == 0:
                first, last = xlow[1, :, 0:8], xlow[1, :, ny - 8 : ny]
            elif start == nx - 4:
                first, last = xhigh[1, :, 0:8], xhigh[1, :, ny - 8 : ny]
            else:
                first = scaled(start, start + 4, 0, 8)
                last = scaled(start, start + 4, ny - 8, ny)
            for pair in range(2):
                at = start // 2 + pair
                ylow[kind, at] = jnp.concatenate([first[2 * pair, 0:4], first[2 * pair + 1, 0:4]], 0)
                yhigh[kind, at] = jnp.concatenate([last[2 * pair, 4:8], last[2 * pair + 1, 4:8]], 0)


def local_kernel(
    codes, mean, logs, noise, wave, wave_prev, adjoint, adjoint_next, bands,
    curved, base_wave, base_adjoint, speed, tilt, sample, listed,
    field, plane,
):
    nx, ny, nz = wave.shape
    points = codes.shape[0]
    sources = 16

    def scan(start, stop, at):
        def step(i, count):
            code = codes[i]
            listed[at + count] = i
            return count + (code >= 0).astype(jnp.int32)

        return lax.fori_loop(start, stop, step, jnp.int32(0), unroll=8)

    n_sources = scan(0, sources, 0)
    n_receivers = scan(sources, points, sources + 1)
    listed[points + 2] = n_sources
    listed[points + 3] = n_receivers

    for kind in range(2):
        field[kind, 0:4] = jnp.zeros((4, ny + 16, nz), F32)
        field[kind, nx + 4 : nx + 8] = jnp.zeros((4, ny + 16, nz), F32)
        field[kind, :, 0:8] = jnp.zeros((nx + 8, 8, nz), F32)
        field[kind, :, ny + 8 : ny + 16] = jnp.zeros((nx + 8, 8, nz), F32)

    def prepare(x, _):
        spread_noise = jnp.exp(logs[x]) * noise[x]
        value = mean[x] + spread_noise
        rate = COURANT_SQUARED * jnp.exp(2.0 * VELOCITY_GAIN * value)
        tilt[x] = spread_noise
        sample[x] = value
        speed[x] = rate
        field[0, x + 4, 8 : ny + 8] = wave[x]
        field[1, x + 4, 8 : ny + 8] = rate * adjoint[x]
        return 0

    lax.fori_loop(0, nx, prepare, 0)

    for kind in range(2):
        value = field[kind, 4 : nx + 4, 8 : ny + 8].reshape(nx * ny, nz)
        plane[kind] = lax.dot_general(
            value, bands[...], ROW, precision=lax.Precision.HIGHEST, preferred_element_type=F32
        )

    def lateral(kind, x):
        total = plane[kind, pl.ds(pl.multiple_of(x * ny, ny), ny)]
        for offset in range(1, 5):
            near = field[kind, x + 4 + offset, 8 : ny + 8] + field[kind, x + 4 - offset, 8 : ny + 8]
            near = near + field[kind, x + 4, 8 + offset : ny + 8 + offset]
            near = near + field[kind, x + 4, 8 - offset : ny + 8 - offset]
            total = total + STENCIL_WEIGHTS[offset] * near
        return total

    def finish(x, _):
        bend = lateral(0, x)
        curved[x] = bend
        base_wave[x] = 2.0 * wave[x] - wave_prev[x] + speed[x] * bend
        base_adjoint[x] = 2.0 * adjoint[x] - adjoint_next[x] + lateral(1, x)
        return 0

    lax.fori_loop(0, nx, finish, 0)


def finish_kernel(
    codes, listed, observed, scalars, curved, base_wave, base_adjoint, speed, tilt,
    xlow, xhigh, ylow, yhigh, forward_z,
    wave_next, adjoint_prev, logscale_grad, spectra,
    slope,
):
    nx, ny, nz = curved.shape
    points = codes.shape[0]
    sources = 16
    row_at = lax.broadcasted_iota(jnp.int32, (8, nz), 0)
    lane_at = lax.broadcasted_iota(jnp.int32, (1, nz), 1)
    keep = [scalars[i] for i in range(4)]
    pulse = scalars[4]

    def lateral_y(kind, x):
        start = jnp.zeros((8, nz), F32)
        end = jnp.zeros((8, nz), F32)
        low, high = ylow[kind, x // 2], yhigh[kind, x // 2]
        mine = row_at < 4 if x % 2 == 0 else row_at >= 4
        low, high = jnp.where(mine, low, 0.0), jnp.where(mine, high, 0.0)
        base = 0 if x % 2 == 0 else 4
        for offset in range(1, 5):
            start = start + STENCIL_WEIGHTS[offset] * pltpu.roll(low, (offset - 4 - base) % 8, 0)
            end = end + STENCIL_WEIGHTS[offset] * pltpu.roll(high, (8 - offset - base) % 8, 0)
        return jnp.where(row_at < 4, start, 0.0) * keep[2], jnp.where(row_at >= 4, end, 0.0) * keep[3]

    def change(kind, x):
        start, end = lateral_y(kind, x)
        total = jnp.concatenate([start, jnp.zeros((ny - 16, nz), F32), end], 0)
        side = None
        for offset in range(1, 5):
            if x - offset < 0:
                term = STENCIL_WEIGHTS[offset] * keep[0] * xlow[kind, x - offset + 4]
            elif x + offset >= nx:
                term = STENCIL_WEIGHTS[offset] * keep[1] * xhigh[kind, x + offset - nx]
            else:
                continue
            total = total + term
        return total

    for x in range(nx):
        more = change(0, x)
        bend = curved[x] + more
        rows = slice(x * ny, (x + 1) * ny)
        wave_next[rows] = base_wave[x] + speed[x] * more
        adjoint_prev[rows] = base_adjoint[x] + change(1, x)
        slope[rows] = (2.0 * VELOCITY_GAIN) * speed[x] * bend

    def shoot(i, _):
        code = codes[listed[i]]
        row = code // nz
        hit = lane_at == code % nz
        wave_next[pl.ds(row, 1)] = wave_next[pl.ds(row, 1)] + jnp.where(hit, pulse, 0.0)
        return 0

    lax.fori_loop(0, listed[points + 2], shoot, 0)

    def record(i, _):
        point = listed[sources + 1 + i]
        code = codes[point]
        row = code // nz
        hit = lane_at == code % nz
        misfit = wave_next[pl.ds(row, 1)] - observed[point - sources]
        adjoint_prev[pl.ds(row, 1)] = adjoint_prev[pl.ds(row, 1)] + jnp.where(hit, misfit, 0.0)
        return 0

    lax.fori_loop(0, listed[points + 3], record, 0)

    matrix = (forward_z[0], forward_z[1])
    for j in range(nx // 2):
        rows = slice(2 * j * ny, 2 * (j + 1) * ny)
        grad = slope[rows] * adjoint_prev[rows]
        logscale_grad[rows] = grad * tilt[2 * j : 2 * j + 2].reshape(2 * ny, nz) - 1.0
        spectra[pl.ds(j, nz, stride=8)] = dot_3(matrix, split(grad), TRANSPOSED_RIGHT)


def filter_kernel(scalars, spectra, matrix_y, matrix_x, terms_x, terms_y, result, plane):
    half = plane.shape[0] // 2
    tiles_x, tiles_y = spectra.shape[0], spectra.shape[1]
    lane = lax.broadcasted_iota(jnp.int32, (half, 128), 1)
    for m in range(tiles_y // 2):
        even = spectra[:, 2 * m].reshape(half, 128)
        odd = spectra[:, 2 * m + 1].reshape(half, 128)
        columns = slice(128 * m, 128 * (m + 1))
        plane[0:half, columns] = jnp.where(lane < 64, even, pltpu.roll(odd, 64, 1))
        plane[half:, columns] = jnp.where(lane < 64, pltpu.roll(even, 64, 1), odd)
    pair_y = (matrix_y[0], matrix_y[1])
    pair_x = (matrix_x[0], matrix_x[1])
    value = dot_3(split(plane[...]), pair_y)
    value = dot_3(pair_x, split(value))
    value = value * (scalars[0] / ((scalars[1] + terms_x[...]) + terms_y[...]))
    value = dot_3(pair_x, split(value), TRANSPOSED_LEFT)
    plane[...] = dot_3(split(value), pair_y)
    for m in range(tiles_y // 2):
        columns = slice(128 * m, 128 * (m + 1))
        even, odd = plane[0:half, columns], plane[half:, columns]
        first = jnp.where(lane < 64, even, pltpu.roll(odd, 64, 1))
        second = jnp.where(lane < 64, pltpu.roll(even, 64, 1), odd)
        result[:, 2 * m] = first.reshape(tiles_x, 8, 128)
        result[:, 2 * m + 1] = second.reshape(tiles_x, 8, 128)


def back_kernel(spectra, inverse_z, sample, search):
    nx, ny, nz = sample.shape
    matrix = (inverse_z[0], inverse_z[1])
    for j in range(nx // 2):
        value = split(spectra[pl.ds(j, nz, stride=8)])
        smooth = dot_3(value, matrix, TRANSPOSED_LEFT)
        search[2 * j : 2 * j + 2] = smooth.reshape(2, ny, nz) + sample[2 * j : 2 * j + 2]


SMEM = pl.BlockSpec(memory_space=pltpu.SMEM)
VMEM = pl.BlockSpec(memory_space=pltpu.VMEM)


def shape(*sizes):
    return jax.ShapeDtypeStruct(sizes, F32)


def per_device(
    mean_field,
    log_scale,
    noise,
    wave_prev,
    wave_now,
    adjoint_next,
    adjoint_now,
    sources,
    receivers,
    observed,
    step_index,
    prior_scale,
):
    nx, ny, nz = wave_now.shape
    parts_x, parts_y = lax.axis_size("gx"), lax.axis_size("gy")
    index_x, index_y = lax.axis_index("gx"), lax.axis_index("gy")
    total_x, total_y = nx * parts_x, ny * parts_y
    block = shape(nx, ny, nz)
    flat = shape(nx * ny, nz)

    xlow, xhigh, ylow, yhigh = pl.pallas_call(
        edges_kernel,
        out_shape=(shape(2, 4, ny, nz),) * 2 + (shape(2, nx // 2, 8, nz),) * 2,
        in_specs=[VMEM] * 5,
        out_specs=(VMEM,) * 4,
        name="edges",
    )(mean_field, log_scale, noise, adjoint_now, wave_now)

    up_x = [(i, (i + 1) % parts_x) for i in range(parts_x)]
    down_x = [(j, i) for i, j in up_x]
    up_y = [(i, (i + 1) % parts_y) for i in range(parts_y)]
    down_y = [(j, i) for i, j in up_y]
    from_low_x = lax.ppermute(xhigh, "gx", up_x)
    from_high_x = lax.ppermute(xlow, "gx", down_x)
    from_low_y = lax.ppermute(yhigh, "gy", up_y)
    from_high_y = lax.ppermute(ylow, "gy", down_y)

    points = jnp.concatenate([sources, receivers], axis=0)
    at_x = points[:, 0] - index_x * nx
    at_y = points[:, 1] - index_y * ny
    inside = (at_x >= 0) & (at_x < nx) & (at_y >= 0) & (at_y < ny)
    codes = jnp.where(inside, (at_x * ny + at_y) * nz + points[:, 2], -1)
    n_points = points.shape[0]

    moment = (step_index[0] - NSTEPS // 2).astype(F32) * (math.pi * PULSE_FREQUENCY)
    pulse = PULSE_AMPLITUDE * (1.0 - 2.0 * moment * moment) * jnp.exp(-moment * moment)
    scalars = jnp.stack(
        [
            (index_x > 0).astype(F32),
            (index_x < parts_x - 1).astype(F32),
            (index_y > 0).astype(F32),
            (index_y < parts_y - 1).astype(F32),
            pulse,
        ]
    )

    bands = jnp.asarray(band(nz).astype(np.float32))
    curved, base_wave, base_adjoint, speed, tilt, sample, listed = pl.pallas_call(
        local_kernel,
        out_shape=(block,) * 6 + (jax.ShapeDtypeStruct((n_points + 4,), jnp.int32),),
        in_specs=[SMEM] + [VMEM] * 8,
        out_specs=(VMEM,) * 6 + (SMEM,),
        scratch_shapes=[
            pltpu.VMEM((2, nx + 8, ny + 16, nz), F32),
            pltpu.VMEM((2, nx * ny, nz), F32),
        ],
        name="local",
    )(codes, mean_field, log_scale, noise, wave_now, wave_prev, adjoint_now, adjoint_next, bands)

    matrix_z = hartley(nz)
    forward_z = jnp.asarray(halves(matrix_z))
    wave_next, adjoint_prev, logscale_grad, spectra = pl.pallas_call(
        finish_kernel,
        out_shape=(flat,) * 4,
        in_specs=[SMEM] * 4 + [VMEM] * 10,
        out_specs=(VMEM,) * 4,
        scratch_shapes=[pltpu.VMEM((nx * ny, nz), F32)],
        name="finish",
    )(
        codes, listed, observed, scalars, curved, base_wave, base_adjoint, speed, tilt,
        from_low_x, from_high_x, from_low_y, from_high_y, forward_z,
    )

    spectra = lax.all_to_all(
        spectra.reshape(nz, 8, nz), ("gx", "gy"), split_axis=0, concat_axis=0, tiled=True
    )

    order = np.arange(total_x).reshape(parts_x, nx // 2, 2).transpose(2, 0, 1).reshape(-1)
    matrix_x = jnp.asarray(halves(hartley(total_x)[:, order]))
    matrix_y = jnp.asarray(halves(hartley(total_y)))
    terms_x = jnp.asarray(wave_terms(total_x).astype(np.float32)[:, None])
    terms_y = jnp.asarray(wave_terms(total_y).astype(np.float32)[None, :])
    terms_z = jnp.asarray(wave_terms(nz).astype(np.float32))
    depth_term = lax.dynamic_index_in_dim(terms_z, index_x * parts_y + index_y, keepdims=False)
    cells = total_x * total_y * nz
    gain = jnp.stack([prior_scale[0] * (math.sqrt(cells) / 8.0 / cells), 1.0 + depth_term])
    filtered = pl.pallas_call(
        filter_kernel,
        out_shape=shape(parts_x, parts_y, 8, nz),
        in_specs=[SMEM] + [VMEM] * 5,
        out_specs=VMEM,
        scratch_shapes=[pltpu.VMEM((total_x, total_y), F32)],
        name="filter",
    )(gain, spectra.reshape(parts_x, parts_y, 8, nz), matrix_y, matrix_x, terms_x, terms_y)

    filtered = lax.all_to_all(
        filtered.reshape(nz, 8, nz), ("gx", "gy"), split_axis=0, concat_axis=0, tiled=True
    )
    search = pl.pallas_call(
        back_kernel,
        out_shape=block,
        in_specs=[VMEM] * 3,
        out_specs=VMEM,
        name="back",
    )(filtered.reshape(nx * ny, nz), forward_z, sample)
    return (
        wave_next.reshape(nx, ny, nz),
        adjoint_prev.reshape(nx, ny, nz),
        search,
        logscale_grad.reshape(nx, ny, nz),
    )


def solution(mesh):
    grid = P("gx", "gy", None)
    return jax.shard_map(
        per_device,
        mesh=mesh,
        in_specs=(grid,) * 7 + (P(),) * 5,
        out_specs=(grid,) * 4,
        check_vma=False,
    )
```

```python
import functools
import math

import jax
import jax.numpy as jnp
import numpy as np
from jax import lax
from jax.experimental import pallas as pl
from jax.experimental.pallas import tpu as pltpu
from jax.sharding import PartitionSpec as P

NSTEPS = 48
STENCIL_WEIGHTS = (-205.0 / 72.0, 8.0 / 5.0, -1.0 / 5.0, 8.0 / 315.0, -1.0 / 560.0)
COURANT_SQUARED = 0.08
VELOCITY_GAIN = 0.2
PULSE_FREQUENCY = 0.05
PULSE_AMPLITUDE = 20.0

F32 = jnp.float32
BF16 = jnp.bfloat16
ROW = (((1,), (0,)), ((), ()))
TRANSPOSED_RIGHT = (((1,), (1,)), ((), ()))
TRANSPOSED_LEFT = (((0,), (0,)), ((), ()))


def hartley(length):
    index = np.arange(length)
    angle = (index[:, None] * index[None, :] % length) * (2.0 * np.pi / length)
    return np.cos(angle) + np.sin(angle)


def halves(matrix):
    high = matrix.astype(np.float32).astype(jnp.bfloat16)
    low = (matrix - high.astype(np.float64)).astype(np.float32).astype(jnp.bfloat16)
    return np.stack([high, low])


def wave_terms(length):
    return (length / 8.0) ** 2 * 4.0 * np.sin(np.arange(length) * (np.pi / length)) ** 2


def band(length):
    matrix = np.zeros((length, length))
    for offset in range(5):
        weight = STENCIL_WEIGHTS[offset] * (3.0 if offset == 0 else 1.0)
        matrix += weight * np.eye(length, k=offset)
        if offset:
            matrix += weight * np.eye(length, k=-offset)
    return matrix


def split(value):
    high = value.astype(BF16)
    return high, (value - high.astype(F32)).astype(BF16)


def dot(left, right, dims=ROW):
    return lax.dot_general(left, right, dims, preferred_element_type=F32)


def dot_3(left, right, dims=ROW):
    total = dot(left[0], right[1], dims) + dot(left[1], right[0], dims)
    return total + dot(left[0], right[0], dims)


def edges_kernel(
    mean, logs, noise, adjoint, wave, xlow, xhigh, ylow, yhigh, ends, starts, stops, sems
):
    nx, ny, _ = wave.shape
    arrays = (mean, logs, noise, adjoint, wave)
    middle = slice(4, nx - 4)
    copies = []
    for i, array in enumerate(arrays):
        low, high = (xlow.at[0], xhigh.at[0]) if i == 4 else (ends.at[i, 0], ends.at[i, 1])
        copies.append(
            (
                pltpu.make_async_copy(array.at[0:4], low, sems.at[i, 0]),
                pltpu.make_async_copy(array.at[nx - 4 : nx], high, sems.at[i, 1]),
                pltpu.make_async_copy(array.at[middle, 0:8], starts.at[i], sems.at[i, 2]),
                pltpu.make_async_copy(array.at[middle, ny - 8 : ny], stops.at[i], sems.at[i, 3]),
            )
        )
    for part in range(4):
        for i in range(5):
            copies[i][part].start()

    def scaled(a, b, c, d):
        return COURANT_SQUARED * jnp.exp(2.0 * VELOCITY_GAIN * (a + jnp.exp(b) * c)) * d

    def pack(kind, base, first, last):
        for pair in range(first.shape[0] // 2):
            at = base // 2 + pair
            ylow[kind, at] = jnp.concatenate([first[2 * pair, 0:4], first[2 * pair + 1, 0:4]], 0)
            yhigh[kind, at] = jnp.concatenate([last[2 * pair, 4:8], last[2 * pair + 1, 4:8]], 0)

    for part, (side, base) in enumerate(((xlow, 0), (xhigh, nx - 4))):
        for i in range(5):
            copies[i][part].wait()
        side[1] = scaled(*(ends[i, part] for i in range(4)))
        for kind in range(2):
            pack(kind, base, side[kind, :, 0:8], side[kind, :, ny - 8 : ny])
    for part in range(2, 4):
        for i in range(5):
            copies[i][part].wait()
    pack(0, 4, starts[4], stops[4])
    pack(1, 4, scaled(*(starts[i] for i in range(4))), scaled(*(stops[i] for i in range(4))))


def local_kernel(
    sources_from, receivers_from, observed_from, wave_prev_from, adjoint_next_from, bands_from,
    mean, logs, noise, wave, adjoint,
    curved, base_wave, base_adjoint, speed, tilt, codes, records, counts,
    field, plane, sources, receivers, observed, wave_prev, adjoint_next, bands, sems,
):
    nx, ny, nz = wave.shape
    index_x, index_y = lax.axis_index("gx"), lax.axis_index("gy")
    n_sources, n_receivers = sources.shape[1], receivers.shape[1]
    copies = [
        pltpu.make_async_copy(sources_from, sources, sems.at[0]),
        pltpu.make_async_copy(receivers_from, receivers, sems.at[1]),
        pltpu.make_async_copy(observed_from, observed, sems.at[2]),
        pltpu.make_async_copy(wave_prev_from, wave_prev, sems.at[3]),
        pltpu.make_async_copy(adjoint_next_from, adjoint_next, sems.at[4]),
        pltpu.make_async_copy(bands_from, bands, sems.at[5]),
    ]
    for copy in copies:
        copy.start()

    def scan(points, start, number, at, count, recorded):
        for i in range(number):
            mine_x = points[0, start + i] - index_x * nx
            mine_y = points[1, start + i] - index_y * ny
            inside = (mine_x >= 0) & (mine_x < nx) & (mine_y >= 0) & (mine_y < ny)
            codes[at + count] = (mine_x * ny + mine_y) * nz + points[2, start + i]
            if recorded:
                records[count] = observed[start + i]
            count = count + inside.astype(jnp.int32)
        return count

    for kind in range(2):
        field[kind, 0:4] = jnp.zeros((4, ny + 16, nz), F32)
        field[kind, nx + 4 : nx + 8] = jnp.zeros((4, ny + 16, nz), F32)
        field[kind, :, 0:8] = jnp.zeros((nx + 8, 8, nz), F32)
        field[kind, :, ny + 8 : ny + 16] = jnp.zeros((nx + 8, 8, nz), F32)

    def prepare(x, _):
        spread_noise = jnp.exp(logs[x]) * noise[x]
        value = mean[x] + spread_noise
        rate = COURANT_SQUARED * jnp.exp(2.0 * VELOCITY_GAIN * value)
        tilt[x] = spread_noise
        speed[x] = rate
        field[0, x + 4, 8 : ny + 8] = wave[x]
        field[1, x + 4, 8 : ny + 8] = rate * adjoint[x]
        return 0

    lax.fori_loop(0, nx, prepare, 0)

    copies[5].wait()
    for kind in range(2):
        value = field[kind, 4 : nx + 4, 8 : ny + 8].reshape(nx * ny, nz)
        plane[kind] = lax.dot_general(
            value, bands[...], ROW, precision=lax.Precision.HIGHEST, preferred_element_type=F32
        )

    def lateral(kind, x):
        total = plane[kind, pl.ds(pl.multiple_of(x * ny, ny), ny)]
        for offset in range(1, 5):
            near = field[kind, x + 4 + offset, 8 : ny + 8] + field[kind, x + 4 - offset, 8 : ny + 8]
            near = near + field[kind, x + 4, 8 + offset : ny + 8 + offset]
            near = near + field[kind, x + 4, 8 - offset : ny + 8 - offset]
            total = total + STENCIL_WEIGHTS[offset] * near
        return total

    for copy in copies[:5]:
        copy.wait()

    def finish(x, count):
        bend = lateral(0, x)
        curved[x] = bend
        base_wave[x] = 2.0 * wave[x] - wave_prev[x] + speed[x] * bend
        base_adjoint[x] = 2.0 * adjoint[x] - adjoint_next[x] + lateral(1, x)
        step = n_sources // nx
        some = scan(sources, x * step, step, 0, count[0], False)
        step = n_receivers // nx
        return some, scan(receivers, x * step, step, n_sources + 1, count[1], True)

    found = lax.fori_loop(0, nx, finish, (jnp.int32(0), jnp.int32(0)))
    counts[0], counts[1] = found


def finish_kernel(
    codes, records, counts, step_index,
    curved, base_wave, base_adjoint, speed, tilt,
    xlow, xhigh, ylow, yhigh, forward_z,
    wave_to, adjoint_to, logscale_to, spectra_to,
    wave_next, adjoint_prev, logscale_grad, slope, spectra, sems,
):
    nx, ny, nz = curved.shape
    index_x, index_y = lax.axis_index("gx"), lax.axis_index("gy")
    n_sources = codes.shape[0] - records.shape[0] - 1
    row_at = lax.broadcasted_iota(jnp.int32, (8, nz), 0)
    lane_at = lax.broadcasted_iota(jnp.int32, (1, nz), 1)
    keep = [
        index_x > 0,
        index_x < lax.axis_size("gx") - 1,
        index_y > 0,
        index_y < lax.axis_size("gy") - 1,
    ]
    keep = [value.astype(F32) for value in keep]
    moment = jnp.full((1, nz), step_index[0] - NSTEPS // 2).astype(F32)
    moment = moment * (math.pi * PULSE_FREQUENCY)
    pulse = PULSE_AMPLITUDE * (1.0 - 2.0 * moment * moment) * jnp.exp(-moment * moment)

    def lateral_y(kind, x):
        start = jnp.zeros((8, nz), F32)
        end = jnp.zeros((8, nz), F32)
        low, high = ylow[kind, x // 2], yhigh[kind, x // 2]
        mine = row_at < 4 if x % 2 == 0 else row_at >= 4
        low, high = jnp.where(mine, low, 0.0), jnp.where(mine, high, 0.0)
        base = 0 if x % 2 == 0 else 4
        for offset in range(1, 5):
            start = start + STENCIL_WEIGHTS[offset] * pltpu.roll(low, (offset - 4 - base) % 8, 0)
            end = end + STENCIL_WEIGHTS[offset] * pltpu.roll(high, (8 - offset - base) % 8, 0)
        return jnp.where(row_at < 4, start, 0.0) * keep[2], jnp.where(row_at >= 4, end, 0.0) * keep[3]

    def change(kind, x):
        start, end = lateral_y(kind, x)
        total = jnp.concatenate([start, jnp.zeros((ny - 16, nz), F32), end], 0)
        side = None
        for offset in range(1, 5):
            if x - offset < 0:
                term = STENCIL_WEIGHTS[offset] * keep[0] * xlow[kind, x - offset + 4]
            elif x + offset >= nx:
                term = STENCIL_WEIGHTS[offset] * keep[1] * xhigh[kind, x + offset - nx]
            else:
                continue
            total = total + term
        return total

    for x in range(nx):
        more = change(0, x)
        bend = curved[x] + more
        rows = slice(x * ny, (x + 1) * ny)
        wave_next[rows] = base_wave[x] + speed[x] * more
        adjoint_prev[rows] = base_adjoint[x] + change(1, x)
        slope[rows] = (2.0 * VELOCITY_GAIN) * speed[x] * bend

    def place(at):
        return pl.ds(codes[at] // nz, 1), lane_at == codes[at] % nz

    def shoot(i, _):
        row, hit = place(i)
        wave_next[row] = wave_next[row] + jnp.where(hit, pulse, 0.0)
        return 0

    lax.fori_loop(0, counts[0], shoot, 0)

    def record(i, _):
        row, hit = place(n_sources + 1 + i)
        misfit = wave_next[row] - records[i]
        adjoint_prev[row] = adjoint_prev[row] + jnp.where(hit, misfit, 0.0)
        return 0

    lax.fori_loop(0, counts[1], record, 0)

    copies = [
        pltpu.make_async_copy(wave_next, wave_to, sems.at[0]),
        pltpu.make_async_copy(adjoint_prev, adjoint_to, sems.at[1]),
    ]
    for copy in copies:
        copy.start()
    matrix = (forward_z[0], forward_z[1])
    for j in range(nx // 2):
        rows = slice(2 * j * ny, 2 * (j + 1) * ny)
        grad = slope[rows] * adjoint_prev[rows]
        logscale_grad[rows] = grad * tilt[2 * j : 2 * j + 2].reshape(2 * ny, nz) - 1.0
        spectra[pl.ds(j, nz, stride=8)] = dot_3(matrix, split(grad), TRANSPOSED_RIGHT)
        copy = pltpu.make_async_copy(logscale_grad.at[rows], logscale_to.at[rows], sems.at[3 + j])
        copy.start()
        copies.append(copy)
    copies.append(pltpu.make_async_copy(spectra, spectra_to, sems.at[2]))
    copies[-1].start()
    for copy in copies:
        copy.wait()


def gain_kernel(
    prior_scale, terms_z, after, matrix_y_from, matrix_x_from, mean_from, terms_x, terms_y, tilt,
    gain, matrix_y, matrix_x, sample, sems,
):
    copies = [
        pltpu.make_async_copy(matrix_y_from, matrix_y, sems.at[0]),
        pltpu.make_async_copy(matrix_x_from, matrix_x, sems.at[1]),
        pltpu.make_async_copy(mean_from, sample, sems.at[2]),
    ]
    for copy in copies:
        copy.start()
    depth = lax.axis_index("gx") * lax.axis_size("gy") + lax.axis_index("gy")
    cells = gain.shape[0] * gain.shape[1] * terms_z.shape[0]
    scale = prior_scale[0] * (math.sqrt(cells) / 8.0 / cells)
    gain[...] = scale / (((1.0 + terms_z[depth]) + terms_x[...]) + terms_y[...])
    for copy in copies:
        copy.wait()
    sample[...] = sample[...] + tilt[...]


def filter_kernel(spectra, matrix_y, matrix_x, gain, result, plane):
    half = plane.shape[0] // 2
    tiles_x, tiles_y = spectra.shape[0], spectra.shape[1]
    lane = lax.broadcasted_iota(jnp.int32, (half, 128), 1)
    for m in range(tiles_y // 2):
        even = spectra[:, 2 * m].reshape(half, 128)
        odd = spectra[:, 2 * m + 1].reshape(half, 128)
        columns = slice(128 * m, 128 * (m + 1))
        plane[0:half, columns] = jnp.where(lane < 64, even, pltpu.roll(odd, 64, 1))
        plane[half:, columns] = jnp.where(lane < 64, pltpu.roll(even, 64, 1), odd)
    pair_y = (matrix_y[0], matrix_y[1])
    pair_x = (matrix_x[0], matrix_x[1])
    value = dot_3(split(plane[...]), pair_y)
    value = dot_3(pair_x, split(value))
    value = value * gain[...]
    value = dot_3(pair_x, split(value), TRANSPOSED_LEFT)
    plane[...] = dot_3(split(value), pair_y)
    for m in range(tiles_y // 2):
        columns = slice(128 * m, 128 * (m + 1))
        even, odd = plane[0:half, columns], plane[half:, columns]
        first = jnp.where(lane < 64, even, pltpu.roll(odd, 64, 1))
        second = jnp.where(lane < 64, pltpu.roll(even, 64, 1), odd)
        result[:, 2 * m] = first.reshape(tiles_x, 8, 128)
        result[:, 2 * m + 1] = second.reshape(tiles_x, 8, 128)


def back_kernel(spectra, inverse_z, sample, search_to, search, sems):
    nx, ny, nz = sample.shape
    matrix = (inverse_z[0], inverse_z[1])
    copies = []
    for j in range(nx // 2):
        value = split(spectra[pl.ds(j, nz, stride=8)])
        smooth = dot_3(value, matrix, TRANSPOSED_LEFT)
        pair = slice(2 * j, 2 * j + 2)
        search[pair] = smooth.reshape(2, ny, nz) + sample[pair]
        copies.append(pltpu.make_async_copy(search.at[pair], search_to.at[pair], sems.at[j]))
        copies[-1].start()
    for copy in copies:
        copy.wait()


SMEM = pl.BlockSpec(memory_space=pltpu.SMEM)
VMEM = pl.BlockSpec(memory_space=pltpu.VMEM)
HBM = pl.BlockSpec(memory_space=pltpu.HBM)


def far(*sizes):
    return jax.ShapeDtypeStruct(sizes, F32)


def near(*sizes):
    return pltpu.VMEM(sizes, F32)


def call(kernel, scalars, stay, arrays, out_shape, out_specs, scratch, name):
    stay = [pltpu.with_memory_space_constraint(value, pltpu.HBM) for value in stay]
    arrays = [pltpu.with_memory_space_constraint(value, pltpu.VMEM) for value in arrays]
    return pl.pallas_call(
        kernel,
        out_shape=out_shape,
        in_specs=[SMEM] * len(scalars) + [HBM] * len(stay) + [VMEM] * len(arrays),
        out_specs=out_specs,
        scratch_shapes=scratch,
        compiler_params=pltpu.CompilerParams(vmem_limit_bytes=16 << 20),
        name=name,
    )(*scalars, *stay, *arrays)


def per_device(
    mean_field,
    log_scale,
    noise,
    wave_prev,
    wave_now,
    adjoint_next,
    adjoint_now,
    sources,
    receivers,
    observed,
    step_index,
    prior_scale,
):
    nx, ny, nz = wave_now.shape
    parts_x, parts_y = lax.axis_size("gx"), lax.axis_size("gy")
    total_x, total_y = nx * parts_x, ny * parts_y
    block = near(nx, ny, nz)
    flat = near(nx * ny, nz)

    edge = near(2, 4, ny, nz), near(2, nx // 2, 8, nz)
    xlow, xhigh, ylow, yhigh = call(
        edges_kernel,
        (),
        (mean_field, log_scale, noise, adjoint_now, wave_now),
        (),
        (edge[0], edge[0], edge[1], edge[1]),
        (VMEM,) * 4,
        [
            near(4, 2, 4, ny, nz),
            near(5, nx - 8, 8, nz),
            near(5, nx - 8, 8, nz),
            pltpu.SemaphoreType.DMA((5, 4)),
        ],
        "edges",
    )

    up_x = [(i, (i + 1) % parts_x) for i in range(parts_x)]
    down_x = [(j, i) for i, j in up_x]
    up_y = [(i, (i + 1) % parts_y) for i in range(parts_y)]
    down_y = [(j, i) for i, j in up_y]
    from_low_x = lax.ppermute(xhigh, "gx", up_x)
    from_high_x = lax.ppermute(xlow, "gx", down_x)
    from_low_y = lax.ppermute(yhigh, "gy", up_y)
    from_high_y = lax.ppermute(ylow, "gy", down_y)

    sources, receivers = sources.T, receivers.T
    n_sources, n_receivers = sources.shape[1], receivers.shape[1]
    bands = jnp.asarray(band(nz).astype(np.float32))
    curved, base_wave, base_adjoint, speed, tilt, codes, records, counts = call(
        local_kernel,
        (),
        (sources, receivers, observed, wave_prev, adjoint_next, bands),
        (mean_field, log_scale, noise, wave_now, adjoint_now),
        (block,) * 5
        + (
            jax.ShapeDtypeStruct((n_sources + n_receivers + 2,), jnp.int32),
            jax.ShapeDtypeStruct((n_receivers + 1,), F32),
            jax.ShapeDtypeStruct((2,), jnp.int32),
        ),
        (VMEM,) * 5 + (SMEM,) * 3,
        [
            near(2, nx + 8, ny + 16, nz),
            near(2, nx * ny, nz),
            pltpu.SMEM(sources.shape, jnp.int32),
            pltpu.SMEM(receivers.shape, jnp.int32),
            pltpu.SMEM(observed.shape, F32),
            near(nx, ny, nz),
            near(nx, ny, nz),
            near(nz, nz),
            pltpu.SemaphoreType.DMA((6,)),
        ],
        "local",
    )

    matrix_z = jnp.asarray(halves(hartley(nz)))
    wave_next, adjoint_prev, logscale_grad, spectra = call(
        finish_kernel,
        (codes, records, counts, step_index),
        (),
        (
            curved, base_wave, base_adjoint, speed, tilt,
            from_low_x, from_high_x, from_low_y, from_high_y, matrix_z,
        ),
        (pltpu.HBM((nx * ny, nz), F32),) * 4,
        (HBM,) * 4,
        [flat] * 5 + [pltpu.SemaphoreType.DMA((3 + nx // 2,))],
        "finish",
    )

    spectra = lax.all_to_all(
        spectra.reshape(nz, 8, nz), ("gx", "gy"), split_axis=0, concat_axis=0, tiled=True
    )

    order = np.arange(total_x).reshape(parts_x, nx // 2, 2).transpose(2, 0, 1).reshape(-1)
    matrix_x = jnp.asarray(halves(hartley(total_x)[:, order]))
    matrix_y = jnp.asarray(halves(hartley(total_y)))
    terms_x = jnp.asarray(wave_terms(total_x).astype(np.float32)[:, None])
    terms_y = jnp.asarray(wave_terms(total_y).astype(np.float32)[None, :])
    terms_z = jnp.asarray(wave_terms(nz).astype(np.float32))
    gain, matrix_y, matrix_x, sample = call(
        gain_kernel,
        (prior_scale, terms_z),
        (logscale_grad, matrix_y, matrix_x, mean_field),
        (terms_x, terms_y, tilt),
        (
            near(total_x, total_y),
            pltpu.VMEM(matrix_y.shape, BF16),
            pltpu.VMEM(matrix_x.shape, BF16),
            block,
        ),
        (VMEM,) * 4,
        [pltpu.SemaphoreType.DMA((3,))],
        "gain",
    )
    filtered = call(
        filter_kernel,
        (),
        (),
        (spectra.reshape(parts_x, parts_y, 8, nz), matrix_y, matrix_x, gain),
        far(parts_x, parts_y, 8, nz),
        VMEM,
        [near(total_x, total_y)],
        "filter",
    )

    filtered = lax.all_to_all(
        filtered.reshape(nz, 8, nz), ("gx", "gy"), split_axis=0, concat_axis=0, tiled=True
    )
    search = call(
        back_kernel,
        (),
        (),
        (filtered.reshape(nx * ny, nz), matrix_z, sample),
        pltpu.HBM((nx, ny, nz), F32),
        HBM,
        [block, pltpu.SemaphoreType.DMA((nx // 2,))],
        "back",
    )
    return (
        wave_next.reshape(nx, ny, nz),
        adjoint_prev.reshape(nx, ny, nz),
        search,
        logscale_grad.reshape(nx, ny, nz),
    )


def solution(mesh):
    grid = P("gx", "gy", None)
    return jax.shard_map(
        per_device,
        mesh=mesh,
        in_specs=(grid,) * 7 + (P(),) * 5,
        out_specs=(grid,) * 4,
        check_vma=False,
    )
```

```python
import functools
import math

import jax
import jax.numpy as jnp
import numpy as np
from jax import lax
from jax.experimental import pallas as pl
from jax.experimental.pallas import tpu as pltpu
from jax.sharding import PartitionSpec as P

NSTEPS = 48
STENCIL_WEIGHTS = (-205.0 / 72.0, 8.0 / 5.0, -1.0 / 5.0, 8.0 / 315.0, -1.0 / 560.0)
COURANT_SQUARED = 0.08
VELOCITY_GAIN = 0.2
PULSE_FREQUENCY = 0.05
PULSE_AMPLITUDE = 20.0

F32 = jnp.float32
BF16 = jnp.bfloat16
ROW = (((1,), (0,)), ((), ()))
TRANSPOSED_RIGHT = (((1,), (1,)), ((), ()))
TRANSPOSED_LEFT = (((0,), (0,)), ((), ()))


def hartley(length):
    index = np.arange(length)
    angle = (index[:, None] * index[None, :] % length) * (2.0 * np.pi / length)
    return np.cos(angle) + np.sin(angle)


def halves(matrix):
    high = matrix.astype(np.float32).astype(jnp.bfloat16)
    low = (matrix - high.astype(np.float64)).astype(np.float32).astype(jnp.bfloat16)
    return np.stack([high, low])


def wave_terms(length):
    return (length / 8.0) ** 2 * 4.0 * np.sin(np.arange(length) * (np.pi / length)) ** 2


def band(length):
    matrix = np.zeros((length, length))
    for offset in range(5):
        weight = STENCIL_WEIGHTS[offset] * (3.0 if offset == 0 else 1.0)
        matrix += weight * np.eye(length, k=offset)
        if offset:
            matrix += weight * np.eye(length, k=-offset)
    return matrix


def split(value):
    high = value.astype(BF16)
    return high, (value - high.astype(F32)).astype(BF16)


def dot(left, right, dims=ROW):
    return lax.dot_general(left, right, dims, preferred_element_type=F32)


def dot_3(left, right, dims=ROW):
    total = dot(left[0], right[1], dims) + dot(left[1], right[0], dims)
    return total + dot(left[0], right[0], dims)


def edges_kernel(
    sources_from, receivers_from, mean_from, logs_from, noise_from, adjoint_from, wave_from,
    xlow, xhigh, ylow, yhigh, field, speed, tilt, adjoint, sample, codes,
    mean, logs, noise, sources, receivers, sems,
):
    nx, ny, nz = speed.shape
    n_sources, n_receivers = sources.shape[1], receivers.shape[1]
    rows = [slice(0, 4), slice(nx - 4, nx), slice(4, nx - 4)]
    pairs = (
        (mean_from, mean),
        (logs_from, logs),
        (noise_from, noise),
        (adjoint_from, adjoint),
        (wave_from, field.at[0, :, 8 : ny + 8]),
    )
    copies = []
    for part in range(3):
        for i, (source, target) in enumerate(pairs):
            copy = pltpu.make_async_copy(
                source.at[rows[part]], target.at[rows[part]], sems.at[part, i]
            )
            copy.start()
            copies.append(copy)
    tables = [
        pltpu.make_async_copy(sources_from, sources, sems.at[0, 5]),
        pltpu.make_async_copy(receivers_from, receivers, sems.at[1, 5]),
    ]
    for copy in tables:
        copy.start()
    for kind in range(2):
        field[kind, :, 0:8] = jnp.zeros((nx, 8, nz), F32)
        field[kind, :, ny + 8 : ny + 16] = jnp.zeros((nx, 8, nz), F32)

    for part in range(3):
        for copy in copies[5 * part : 5 * part + 5]:
            copy.wait()
        for x in range(rows[part].start, rows[part].stop):
            spread_noise = jnp.exp(logs[x]) * noise[x]
            value = mean[x] + spread_noise
            sample[x] = value
            rate = COURANT_SQUARED * jnp.exp(2.0 * VELOCITY_GAIN * value)
            tilt[x] = spread_noise
            speed[x] = rate
            scaled = rate * adjoint[x]
            field[1, x, 8 : ny + 8] = scaled
            for kind in range(2):
                value = scaled if kind else field[0, x, 8 : ny + 8]
                if part == 0:
                    xlow[kind, x] = value
                elif part == 1:
                    xhigh[kind, x - nx + 4] = value
                half = slice(4 * (x % 2), 4 * (x % 2) + 4)
                ylow[kind, x // 2, half] = value[0:4]
                yhigh[kind, x // 2, half] = value[ny - 4 : ny]

    for copy in tables:
        copy.wait()

    def code(points):
        at_x = points[0:1] - lax.axis_index("gx") * nx
        at_y = points[1:2] - lax.axis_index("gy") * ny
        inside = (at_x >= 0) & (at_x < nx) & (at_y >= 0) & (at_y < ny)
        return jnp.where(inside, (at_x * ny + at_y) * nz + points[2:3], -1)

    codes[:, 0:n_receivers] = code(receivers)
    codes[:, n_receivers : n_receivers + n_sources] = code(sources)


def local_kernel(
    codes, prior_scale, terms_z, wave_prev_from, adjoint_next_from, bands_from, matrix_y_from, matrix_x_from,
    field, speed, adjoint,
    curved, base_wave, base_adjoint, matrix_y, matrix_x, listed, counts, gains,
    plane, wave_prev, adjoint_next, bands, sems,
):
    nx, ny, nz = speed.shape
    n_receivers = counts.shape[0] - 2
    n_sources = listed.shape[0] - 2 - n_receivers
    copies = [
        pltpu.make_async_copy(bands_from, bands, sems.at[0]),
        pltpu.make_async_copy(wave_prev_from, wave_prev, sems.at[1]),
        pltpu.make_async_copy(adjoint_next_from, adjoint_next, sems.at[2]),
        pltpu.make_async_copy(matrix_y_from, matrix_y, sems.at[3]),
        pltpu.make_async_copy(matrix_x_from, matrix_x, sems.at[4]),
    ]
    for copy in copies:
        copy.start()

    def scan(first, number, at, count):
        for i in range(number):
            listed[at + count] = first + i
            count = count + (codes[0, first + i] >= 0).astype(jnp.int32)
        return count

    copies[0].wait()
    pair = (bands[0], bands[1])
    for kind in range(2):
        for x in range(0, nx, 4):
            value = field[kind, x : x + 4, 8 : ny + 8].reshape(4 * ny, nz)
            plane[kind, x : x + 4] = dot_3(split(value), pair).reshape(4, ny, nz)
    for copy in copies[1:3]:
        copy.wait()

    def strip(t, count):
        start = pl.multiple_of(8 * t, 8)
        here = pl.ds(start, 8)
        for kind in range(2):
            centre = [field[kind, x, pl.ds(start + 8, 8)] for x in range(nx)]
            for x in range(nx):
                total = plane[kind, x, here]
                for offset in range(1, 5):
                    near_by = field[kind, x, pl.ds(start + 8 + offset, 8)]
                    near_by = near_by + field[kind, x, pl.ds(start + 8 - offset, 8)]
                    if x + offset < nx:
                        near_by = near_by + centre[x + offset]
                    if x - offset >= 0:
                        near_by = near_by + centre[x - offset]
                    total = total + STENCIL_WEIGHTS[offset] * near_by
                if kind == 0:
                    curved[x, here] = total
                    rest = 2.0 * centre[x] - wave_prev[x, here]
                    base_wave[x, here] = rest + speed[x, here] * total
                else:
                    rest = 2.0 * adjoint[x, here] - adjoint_next[x, here]
                    base_adjoint[x, here] = rest + total
        step = n_receivers // (ny // 8)
        some = scan(t * step, step, n_sources + 1, count[0])
        step = n_sources // (ny // 8)
        return some, scan(n_receivers + t * step, step, 0, count[1])

    found = lax.fori_loop(0, ny // 8, strip, (jnp.int32(0), jnp.int32(0)))
    counts[0], counts[1] = found[1], found[0]
    depth = lax.axis_index("gx") * lax.axis_size("gy") + lax.axis_index("gy")
    cells = matrix_x.shape[1] * matrix_y.shape[1] * nz
    gains[0] = prior_scale[0] * (math.sqrt(cells) / 8.0 / cells)
    gains[1] = 1.0 + terms_z[depth]
    for copy in copies[3:]:
        copy.wait()


def finish_kernel(
    codes, listed, counts, observed, step_index,
    curved, base_wave, base_adjoint, speed, tilt,
    xlow, xhigh, ylow, yhigh, forward_z,
    wave_to, adjoint_to, logscale_to, spectra,
    wave_next, adjoint_prev, logscale_grad, slope, sems,
):
    nx, ny, nz = curved.shape
    index_x, index_y = lax.axis_index("gx"), lax.axis_index("gy")
    n_receivers = counts.shape[0] - 2
    n_sources = listed.shape[0] - 2 - n_receivers
    row_at = lax.broadcasted_iota(jnp.int32, (8, nz), 0)
    lane_at = lax.broadcasted_iota(jnp.int32, (1, nz), 1)
    keep = [
        index_x > 0,
        index_x < lax.axis_size("gx") - 1,
        index_y > 0,
        index_y < lax.axis_size("gy") - 1,
    ]
    keep = [value.astype(F32) for value in keep]
    moment = jnp.full((1, nz), step_index[0] - NSTEPS // 2).astype(F32)
    moment = moment * (math.pi * PULSE_FREQUENCY)
    pulse = PULSE_AMPLITUDE * (1.0 - 2.0 * moment * moment) * jnp.exp(-moment * moment)

    def lateral_y(kind, x):
        start = jnp.zeros((8, nz), F32)
        end = jnp.zeros((8, nz), F32)
        low, high = ylow[kind, x // 2], yhigh[kind, x // 2]
        mine = row_at < 4 if x % 2 == 0 else row_at >= 4
        low, high = jnp.where(mine, low, 0.0), jnp.where(mine, high, 0.0)
        base = 0 if x % 2 == 0 else 4
        for offset in range(1, 5):
            start = start + STENCIL_WEIGHTS[offset] * pltpu.roll(low, (offset - 4 - base) % 8, 0)
            end = end + STENCIL_WEIGHTS[offset] * pltpu.roll(high, (8 - offset - base) % 8, 0)
        return jnp.where(row_at < 4, start, 0.0) * keep[2], jnp.where(row_at >= 4, end, 0.0) * keep[3]

    def change(kind, x):
        start, end = lateral_y(kind, x)
        total = jnp.concatenate([start, jnp.zeros((ny - 16, nz), F32), end], 0)
        side = None
        for offset in range(1, 5):
            if x - offset < 0:
                term = STENCIL_WEIGHTS[offset] * keep[0] * xlow[kind, x - offset + 4]
            elif x + offset >= nx:
                term = STENCIL_WEIGHTS[offset] * keep[1] * xhigh[kind, x + offset - nx]
            else:
                continue
            total = total + term
        return total

    for x in range(nx):
        more = change(0, x)
        bend = curved[x] + more
        rows = slice(x * ny, (x + 1) * ny)
        wave_next[rows] = base_wave[x] + speed[x] * more
        adjoint_prev[rows] = base_adjoint[x] + change(1, x)
        slope[rows] = (2.0 * VELOCITY_GAIN) * speed[x] * bend

    def place(point):
        code = codes[0, point]
        return pl.ds(code // nz, 1), lane_at == code % nz

    def shoot(i, _):
        row, hit = place(listed[i])
        wave_next[row] = wave_next[row] + jnp.where(hit, pulse, 0.0)
        return 0

    lax.fori_loop(0, counts[0], shoot, 0)

    def record(i, _):
        point = listed[n_sources + 1 + i]
        row, hit = place(point)
        misfit = wave_next[row] - observed[point]
        adjoint_prev[row] = adjoint_prev[row] + jnp.where(hit, misfit, 0.0)
        return 0

    lax.fori_loop(0, counts[1], record, 0)

    copies = [
        pltpu.make_async_copy(wave_next, wave_to, sems.at[0]),
        pltpu.make_async_copy(adjoint_prev, adjoint_to, sems.at[1]),
    ]
    for copy in copies:
        copy.start()
    matrix = (forward_z[0], forward_z[1])
    for j in range(nx // 2):
        rows = slice(2 * j * ny, 2 * (j + 1) * ny)
        grad = slope[rows] * adjoint_prev[rows]
        logscale_grad[rows] = grad * tilt[2 * j : 2 * j + 2].reshape(2 * ny, nz) - 1.0
        spectra[pl.ds(j, nz, stride=8)] = dot_3(matrix, split(grad), TRANSPOSED_RIGHT)
        copy = pltpu.make_async_copy(logscale_grad.at[rows], logscale_to.at[rows], sems.at[2 + j])
        copy.start()
        copies.append(copy)
    for copy in copies:
        copy.wait()


def filter_kernel(gains, spectra, matrix_y, matrix_x, terms_x, terms_y, result, plane):
    half = plane.shape[0] // 2
    tiles_x, tiles_y = spectra.shape[0], spectra.shape[1]
    lane = lax.broadcasted_iota(jnp.int32, (half, 128), 1)
    for m in range(tiles_y // 2):
        even = spectra[:, 2 * m].reshape(half, 128)
        odd = spectra[:, 2 * m + 1].reshape(half, 128)
        columns = slice(128 * m, 128 * (m + 1))
        plane[0:half, columns] = jnp.where(lane < 64, even, pltpu.roll(odd, 64, 1))
        plane[half:, columns] = jnp.where(lane < 64, pltpu.roll(even, 64, 1), odd)
    pair_y = (matrix_y[0], matrix_y[1])
    pair_x = (matrix_x[0], matrix_x[1])
    value = dot_3(split(plane[...]), pair_y)
    value = dot_3(pair_x, split(value))
    value = value * (gains[0] / ((gains[1] + terms_x[...]) + terms_y[...]))
    value = dot_3(pair_x, split(value), TRANSPOSED_LEFT)
    plane[...] = dot_3(split(value), pair_y)
    for m in range(tiles_y // 2):
        columns = slice(128 * m, 128 * (m + 1))
        even, odd = plane[0:half, columns], plane[half:, columns]
        first = jnp.where(lane < 64, even, pltpu.roll(odd, 64, 1))
        second = jnp.where(lane < 64, pltpu.roll(even, 64, 1), odd)
        result[:, 2 * m] = first.reshape(tiles_x, 8, 128)
        result[:, 2 * m + 1] = second.reshape(tiles_x, 8, 128)


def back_kernel(spectra, inverse_z, sample, search_to, search, sems):
    nx, ny, nz = sample.shape
    matrix = (inverse_z[0], inverse_z[1])
    copies = []
    for j in range(nx // 2):
        value = split(spectra[pl.ds(j, nz, stride=8)])
        smooth = dot_3(value, matrix, TRANSPOSED_LEFT)
        pair = slice(2 * j, 2 * j + 2)
        search[pair] = smooth.reshape(2, ny, nz) + sample[pair]
        copies.append(pltpu.make_async_copy(search.at[pair], search_to.at[pair], sems.at[j]))
        copies[-1].start()
    for copy in copies:
        copy.wait()


SMEM = pl.BlockSpec(memory_space=pltpu.SMEM)
VMEM = pl.BlockSpec(memory_space=pltpu.VMEM)
HBM = pl.BlockSpec(memory_space=pltpu.HBM)


def far(*sizes):
    return jax.ShapeDtypeStruct(sizes, F32)


def near(*sizes):
    return pltpu.VMEM(sizes, F32)


def call(kernel, scalars, stay, arrays, out_shape, out_specs, scratch, name):
    stay = [pltpu.with_memory_space_constraint(value, pltpu.HBM) for value in stay]
    arrays = [pltpu.with_memory_space_constraint(value, pltpu.VMEM) for value in arrays]
    return pl.pallas_call(
        kernel,
        out_shape=out_shape,
        in_specs=[SMEM] * len(scalars) + [HBM] * len(stay) + [VMEM] * len(arrays),
        out_specs=out_specs,
        scratch_shapes=scratch,
        compiler_params=pltpu.CompilerParams(vmem_limit_bytes=16 << 20),
        name=name,
    )(*scalars, *stay, *arrays)


def per_device(
    mean_field,
    log_scale,
    noise,
    wave_prev,
    wave_now,
    adjoint_next,
    adjoint_now,
    sources,
    receivers,
    observed,
    step_index,
    prior_scale,
):
    nx, ny, nz = wave_now.shape
    parts_x, parts_y = lax.axis_size("gx"), lax.axis_size("gy")
    total_x, total_y = nx * parts_x, ny * parts_y
    block = near(nx, ny, nz)
    flat = near(nx * ny, nz)

    sources, receivers = sources.T, receivers.T
    n_sources, n_receivers = sources.shape[1], receivers.shape[1]
    edge_x, edge_y = near(2, 4, ny, nz), near(2, nx // 2, 8, nz)
    xlow, xhigh, ylow, yhigh, field, speed, tilt, adjoint, sample, codes = call(
        edges_kernel,
        (),
        (sources, receivers, mean_field, log_scale, noise, adjoint_now, wave_now),
        (),
        (edge_x, edge_x, edge_y, edge_y, near(2, nx, ny + 16, nz), block, block, block, block)
        + (jax.ShapeDtypeStruct((1, n_sources + n_receivers), jnp.int32),),
        (VMEM,) * 10,
        [
            near(nx, ny, nz),
            near(nx, ny, nz),
            near(nx, ny, nz),
            pltpu.VMEM(sources.shape, jnp.int32),
            pltpu.VMEM(receivers.shape, jnp.int32),
            pltpu.SemaphoreType.DMA((3, 6)),
        ],
        "edges",
    )

    up_x = [(i, (i + 1) % parts_x) for i in range(parts_x)]
    down_x = [(j, i) for i, j in up_x]
    up_y = [(i, (i + 1) % parts_y) for i in range(parts_y)]
    down_y = [(j, i) for i, j in up_y]
    from_low_x = lax.ppermute(xhigh, "gx", up_x)
    from_high_x = lax.ppermute(xlow, "gx", down_x)
    from_low_y = lax.ppermute(yhigh, "gy", up_y)
    from_high_y = lax.ppermute(ylow, "gy", down_y)

    order = np.arange(total_x).reshape(parts_x, nx // 2, 2).transpose(2, 0, 1).reshape(-1)
    matrix_x = jnp.asarray(halves(hartley(total_x)[:, order]))
    matrix_y = jnp.asarray(halves(hartley(total_y)))
    terms_z = jnp.asarray(wave_terms(nz).astype(np.float32))
    bands = jnp.asarray(halves(band(nz)))
    curved, base_wave, base_adjoint, matrix_y, matrix_x, listed, counts, gains = call(
        local_kernel,
        (codes, prior_scale, terms_z),
        (wave_prev, adjoint_next, bands, matrix_y, matrix_x),
        (field, speed, adjoint),
        (block,) * 3
        + (
            pltpu.VMEM(matrix_y.shape, BF16),
            pltpu.VMEM(matrix_x.shape, BF16),
            jax.ShapeDtypeStruct((n_sources + n_receivers + 2,), jnp.int32),
            jax.ShapeDtypeStruct((n_receivers + 2,), jnp.int32),
            far(2),
        ),
        (VMEM,) * 5 + (SMEM,) * 3,
        [
            near(2, nx, ny, nz),
            near(nx, ny, nz),
            near(nx, ny, nz),
            pltpu.VMEM(bands.shape, BF16),
            pltpu.SemaphoreType.DMA((5,)),
        ],
        "local",
    )

    matrix_z = jnp.asarray(halves(hartley(nz)))
    wave_next, adjoint_prev, logscale_grad, spectra = call(
        finish_kernel,
        (codes, listed, counts, observed, step_index),
        (),
        (
            curved, base_wave, base_adjoint, speed, tilt,
            from_low_x, from_high_x, from_low_y, from_high_y, matrix_z,
        ),
        (pltpu.HBM((nx * ny, nz), F32),) * 3 + (far(nx * ny, nz),),
        (HBM,) * 3 + (VMEM,),
        [flat] * 4 + [pltpu.SemaphoreType.DMA((2 + nx // 2,))],
        "finish",
    )

    spectra = lax.all_to_all(
        spectra.reshape(nz, 8, nz), ("gx", "gy"), split_axis=0, concat_axis=0, tiled=True
    )

    terms_x = jnp.asarray(wave_terms(total_x).astype(np.float32)[:, None])
    terms_y = jnp.asarray(wave_terms(total_y).astype(np.float32)[None, :])
    filtered = call(
        filter_kernel,
        (gains,),
        (),
        (spectra.reshape(parts_x, parts_y, 8, nz), matrix_y, matrix_x, terms_x, terms_y),
        far(parts_x, parts_y, 8, nz),
        VMEM,
        [near(total_x, total_y)],
        "filter",
    )

    filtered = lax.all_to_all(
        filtered.reshape(nz, 8, nz), ("gx", "gy"), split_axis=0, concat_axis=0, tiled=True
    )
    search = call(
        back_kernel,
        (),
        (),
        (filtered.reshape(nx * ny, nz), matrix_z, sample),
        pltpu.HBM((nx, ny, nz), F32),
        HBM,
        [block, pltpu.SemaphoreType.DMA((nx // 2,))],
        "back",
    )
    return (
        wave_next.reshape(nx, ny, nz),
        adjoint_prev.reshape(nx, ny, nz),
        search,
        logscale_grad.reshape(nx, ny, nz),
    )


def solution(mesh):
    grid = P("gx", "gy", None)
    return jax.shard_map(
        per_device,
        mesh=mesh,
        in_specs=(grid,) * 7 + (P(),) * 5,
        out_specs=(grid,) * 4,
        check_vma=False,
    )
```

```python
import functools
import math

import jax
import jax.numpy as jnp
import numpy as np
from jax import lax
from jax.experimental import pallas as pl
from jax.experimental.pallas import tpu as pltpu
from jax.sharding import PartitionSpec as P

NSTEPS = 48
STENCIL_WEIGHTS = (-205.0 / 72.0, 8.0 / 5.0, -1.0 / 5.0, 8.0 / 315.0, -1.0 / 560.0)
COURANT_SQUARED = 0.08
VELOCITY_GAIN = 0.2
PULSE_FREQUENCY = 0.05
PULSE_AMPLITUDE = 20.0

F32 = jnp.float32
BF16 = jnp.bfloat16
ROW = (((1,), (0,)), ((), ()))
TRANSPOSED_RIGHT = (((1,), (1,)), ((), ()))
TRANSPOSED_LEFT = (((0,), (0,)), ((), ()))


def hartley(length):
    index = np.arange(length)
    angle = (index[:, None] * index[None, :] % length) * (2.0 * np.pi / length)
    return np.cos(angle) + np.sin(angle)


def halves(matrix):
    high = matrix.astype(np.float32).astype(jnp.bfloat16)
    low = (matrix - high.astype(np.float64)).astype(np.float32).astype(jnp.bfloat16)
    return np.stack([high, low])


def wave_terms(length):
    return (length / 8.0) ** 2 * 4.0 * np.sin(np.arange(length) * (np.pi / length)) ** 2


def band(length):
    matrix = np.zeros((length, length))
    for offset in range(5):
        weight = STENCIL_WEIGHTS[offset] * (3.0 if offset == 0 else 1.0)
        matrix += weight * np.eye(length, k=offset)
        if offset:
            matrix += weight * np.eye(length, k=-offset)
    return matrix


def split(value):
    high = value.astype(BF16)
    return high, (value - high.astype(F32)).astype(BF16)


def dot(left, right, dims=ROW):
    return lax.dot_general(left, right, dims, preferred_element_type=F32)


def dot_3(left, right, dims=ROW):
    (on_left,), (on_right,) = dims[0]
    if left[0].shape[on_left] <= 128:
        cross = dot(
            jnp.concatenate(left, axis=on_left), jnp.concatenate(right[::-1], axis=on_right), dims
        )
    else:
        cross = dot(left[0], right[1], dims) + dot(left[1], right[0], dims)
    return cross + dot(left[0], right[0], dims)


def edges_kernel(
    sources_from, receivers_from, mean_from, logs_from, noise_from, adjoint_from, wave_from,
    xlow, xhigh, ylow, yhigh, field, speed, tilt, adjoint, sample, codes,
    mean, logs, noise, sources, receivers, sems,
):
    nx, ny, nz = speed.shape
    n_sources, n_receivers = sources.shape[1], receivers.shape[1]
    rows = [slice(0, 4), slice(nx - 4, nx), slice(4, nx - 4)]
    pairs = (
        (mean_from, mean),
        (logs_from, logs),
        (noise_from, noise),
        (adjoint_from, adjoint),
        (wave_from, field.at[0, :, 8 : ny + 8]),
    )
    copies = []
    for part in range(3):
        for i, (source, target) in enumerate(pairs):
            copy = pltpu.make_async_copy(
                source.at[rows[part]], target.at[rows[part]], sems.at[part, i]
            )
            copy.start()
            copies.append(copy)
    tables = [
        pltpu.make_async_copy(sources_from, sources, sems.at[0, 5]),
        pltpu.make_async_copy(receivers_from, receivers, sems.at[1, 5]),
    ]
    for copy in tables:
        copy.start()
    for kind in range(2):
        field[kind, :, 0:8] = jnp.zeros((nx, 8, nz), F32)
        field[kind, :, ny + 8 : ny + 16] = jnp.zeros((nx, 8, nz), F32)

    for part in range(3):
        for copy in copies[5 * part : 5 * part + 5]:
            copy.wait()
        for x in range(rows[part].start, rows[part].stop):
            spread_noise = jnp.exp(logs[x]) * noise[x]
            value = mean[x] + spread_noise
            sample[x] = value
            rate = COURANT_SQUARED * jnp.exp(2.0 * VELOCITY_GAIN * value)
            tilt[x] = spread_noise
            speed[x] = rate
            scaled = rate * adjoint[x]
            field[1, x, 8 : ny + 8] = scaled
            for kind in range(2):
                value = scaled if kind else field[0, x, 8 : ny + 8]
                if part == 0:
                    xlow[kind, x] = value
                elif part == 1:
                    xhigh[kind, x - nx + 4] = value
                half = slice(4 * (x % 2), 4 * (x % 2) + 4)
                ylow[kind, x // 2, half] = value[0:4]
                yhigh[kind, x // 2, half] = value[ny - 4 : ny]

    for copy in tables:
        copy.wait()

    def code(points):
        at_x = points[0:1] - lax.axis_index("gx") * nx
        at_y = points[1:2] - lax.axis_index("gy") * ny
        inside = (at_x >= 0) & (at_x < nx) & (at_y >= 0) & (at_y < ny)
        return jnp.where(inside, (at_x * ny + at_y) * nz + points[2:3], -1)

    codes[:, 0:n_receivers] = code(receivers)
    codes[:, n_receivers : n_receivers + n_sources] = code(sources)


def local_kernel(
    codes, prior_scale, terms_z, wave_prev_from, adjoint_next_from, bands_from, matrix_y_from, matrix_x_from,
    field, speed, adjoint,
    curved, base_wave, base_adjoint, matrix_y, matrix_x, listed, counts, gains,
    plane, wave_prev, adjoint_next, bands, sems,
):
    nx, ny, nz = speed.shape
    n_receivers = counts.shape[0] - 2
    n_sources = listed.shape[0] - 2 - n_receivers
    copies = [
        pltpu.make_async_copy(bands_from, bands, sems.at[0]),
        pltpu.make_async_copy(wave_prev_from, wave_prev, sems.at[1]),
        pltpu.make_async_copy(adjoint_next_from, adjoint_next, sems.at[2]),
        pltpu.make_async_copy(matrix_y_from, matrix_y, sems.at[3]),
        pltpu.make_async_copy(matrix_x_from, matrix_x, sems.at[4]),
    ]
    for copy in copies:
        copy.start()

    def scan(first, number, at, count):
        for i in range(number):
            listed[at + count] = first + i
            count = count + (codes[0, first + i] >= 0).astype(jnp.int32)
        return count

    copies[0].wait()
    pair = (bands[0], bands[1])
    for kind in range(2):
        for x in range(0, nx, 4):
            value = field[kind, x : x + 4, 8 : ny + 8].reshape(4 * ny, nz)
            plane[kind, x : x + 4] = dot_3(split(value), pair).reshape(4, ny, nz)
    for copy in copies[1:3]:
        copy.wait()

    def strip(t, count):
        start = pl.multiple_of(8 * t, 8)
        here = pl.ds(start, 8)
        for kind in range(2):
            centre = [field[kind, x, pl.ds(start + 8, 8)] for x in range(nx)]
            for x in range(nx):
                total = plane[kind, x, here]
                for offset in range(1, 5):
                    near_by = field[kind, x, pl.ds(start + 8 + offset, 8)]
                    near_by = near_by + field[kind, x, pl.ds(start + 8 - offset, 8)]
                    if x + offset < nx:
                        near_by = near_by + centre[x + offset]
                    if x - offset >= 0:
                        near_by = near_by + centre[x - offset]
                    total = total + STENCIL_WEIGHTS[offset] * near_by
                if kind == 0:
                    curved[x, here] = total
                    rest = 2.0 * centre[x] - wave_prev[x, here]
                    base_wave[x, here] = rest + speed[x, here] * total
                else:
                    rest = 2.0 * adjoint[x, here] - adjoint_next[x, here]
                    base_adjoint[x, here] = rest + total
        step = n_receivers // (ny // 8)
        some = scan(t * step, step, n_sources + 1, count[0])
        step = n_sources // (ny // 8)
        return some, scan(n_receivers + t * step, step, 0, count[1])

    found = lax.fori_loop(0, ny // 8, strip, (jnp.int32(0), jnp.int32(0)))
    counts[0], counts[1] = found[1], found[0]
    depth = lax.axis_index("gx") * lax.axis_size("gy") + lax.axis_index("gy")
    cells = matrix_x.shape[1] * matrix_y.shape[1] * nz
    gains[0] = prior_scale[0] * (math.sqrt(cells) / 8.0 / cells)
    gains[1] = 1.0 + terms_z[depth]
    for copy in copies[3:]:
        copy.wait()


def finish_kernel(
    codes, listed, counts, observed, step_index,
    curved, base_wave, base_adjoint, speed, tilt,
    xlow, xhigh, ylow, yhigh, forward_z,
    wave_to, adjoint_to, logscale_to, spectra,
    wave_next, adjoint_prev, logscale_grad, slope, sems,
):
    nx, ny, nz = curved.shape
    index_x, index_y = lax.axis_index("gx"), lax.axis_index("gy")
    n_receivers = counts.shape[0] - 2
    n_sources = listed.shape[0] - 2 - n_receivers
    row_at = lax.broadcasted_iota(jnp.int32, (8, nz), 0)
    lane_at = lax.broadcasted_iota(jnp.int32, (1, nz), 1)
    keep = [
        index_x > 0,
        index_x < lax.axis_size("gx") - 1,
        index_y > 0,
        index_y < lax.axis_size("gy") - 1,
    ]
    keep = [value.astype(F32) for value in keep]
    moment = jnp.full((1, nz), step_index[0] - NSTEPS // 2).astype(F32)
    moment = moment * (math.pi * PULSE_FREQUENCY)
    pulse = PULSE_AMPLITUDE * (1.0 - 2.0 * moment * moment) * jnp.exp(-moment * moment)

    def lateral_y(kind, x):
        start = jnp.zeros((8, nz), F32)
        end = jnp.zeros((8, nz), F32)
        low, high = ylow[kind, x // 2], yhigh[kind, x // 2]
        mine = row_at < 4 if x % 2 == 0 else row_at >= 4
        low, high = jnp.where(mine, low, 0.0), jnp.where(mine, high, 0.0)
        base = 0 if x % 2 == 0 else 4
        for offset in range(1, 5):
            start = start + STENCIL_WEIGHTS[offset] * pltpu.roll(low, (offset - 4 - base) % 8, 0)
            end = end + STENCIL_WEIGHTS[offset] * pltpu.roll(high, (8 - offset - base) % 8, 0)
        return jnp.where(row_at < 4, start, 0.0) * keep[2], jnp.where(row_at >= 4, end, 0.0) * keep[3]

    def change(kind, x, edges, first, last):
        total = None
        if first == 0:
            total = edges[0]
        elif last == ny:
            total = edges[1]
        for offset in range(1, 5):
            if x - offset < 0:
                layer, weight = xlow[kind, x - offset + 4, first:last], keep[0]
            elif x + offset >= nx:
                layer, weight = xhigh[kind, x + offset - nx, first:last], keep[1]
            else:
                continue
            term = STENCIL_WEIGHTS[offset] * weight * layer
            total = term if total is None else total + term
        return total

    for x in range(nx):
        edges = [lateral_y(kind, x) for kind in range(2)]
        for first, last in ((0, 8), (8, ny - 8), (ny - 8, ny)):
            rows = slice(x * ny + first, x * ny + last)
            bend, rate = curved[x, first:last], speed[x, first:last]
            onward, backward = base_wave[x, first:last], base_adjoint[x, first:last]
            more = change(0, x, edges[0], first, last)
            if more is not None:
                bend, onward = bend + more, onward + rate * more
                backward = backward + change(1, x, edges[1], first, last)
            wave_next[rows] = onward
            adjoint_prev[rows] = backward
            slope[rows] = (2.0 * VELOCITY_GAIN) * rate * bend

    def place(point):
        code = codes[0, point]
        return pl.ds(code // nz, 1), lane_at == code % nz

    def shoot(i, _):
        row, hit = place(listed[i])
        wave_next[row] = wave_next[row] + jnp.where(hit, pulse, 0.0)
        return 0

    lax.fori_loop(0, counts[0], shoot, 0)

    def record(i, _):
        point = listed[n_sources + 1 + i]
        row, hit = place(point)
        misfit = wave_next[row] - observed[point]
        adjoint_prev[row] = adjoint_prev[row] + jnp.where(hit, misfit, 0.0)
        return 0

    lax.fori_loop(0, counts[1], record, 0)

    copies = [
        pltpu.make_async_copy(wave_next, wave_to, sems.at[0]),
        pltpu.make_async_copy(adjoint_prev, adjoint_to, sems.at[1]),
    ]
    for copy in copies:
        copy.start()
    matrix = (forward_z[0], forward_z[1])
    for j in range(nx // 2):
        rows = slice(2 * j * ny, 2 * (j + 1) * ny)
        grad = slope[rows] * adjoint_prev[rows]
        logscale_grad[rows] = grad * tilt[2 * j : 2 * j + 2].reshape(2 * ny, nz) - 1.0
        spectra[pl.ds(j, nz, stride=8)] = dot_3(matrix, split(grad), TRANSPOSED_RIGHT)
        copy = pltpu.make_async_copy(logscale_grad.at[rows], logscale_to.at[rows], sems.at[2 + j])
        copy.start()
        copies.append(copy)
    for copy in copies:
        copy.wait()


def filter_kernel(gains, spectra, matrix_y, matrix_x, terms_x, terms_y, result, plane):
    half = plane.shape[0] // 2
    tiles_x, tiles_y = spectra.shape[0], spectra.shape[1]
    lane = lax.broadcasted_iota(jnp.int32, (half, 128), 1)
    for m in range(tiles_y // 2):
        even = spectra[:, 2 * m].reshape(half, 128)
        odd = spectra[:, 2 * m + 1].reshape(half, 128)
        columns = slice(128 * m, 128 * (m + 1))
        plane[0:half, columns] = jnp.where(lane < 64, even, pltpu.roll(odd, 64, 1))
        plane[half:, columns] = jnp.where(lane < 64, pltpu.roll(even, 64, 1), odd)
    pair_y = (matrix_y[0], matrix_y[1])
    pair_x = (matrix_x[0], matrix_x[1])
    value = dot_3(split(plane[...]), pair_y)
    value = dot_3(pair_x, split(value))
    value = value * (gains[0] / ((gains[1] + terms_x[...]) + terms_y[...]))
    value = dot_3(pair_x, split(value), TRANSPOSED_LEFT)
    plane[...] = dot_3(split(value), pair_y)
    for m in range(tiles_y // 2):
        columns = slice(128 * m, 128 * (m + 1))
        even, odd = plane[0:half, columns], plane[half:, columns]
        first = jnp.where(lane < 64, even, pltpu.roll(odd, 64, 1))
        second = jnp.where(lane < 64, pltpu.roll(even, 64, 1), odd)
        result[:, 2 * m] = first.reshape(tiles_x, 8, 128)
        result[:, 2 * m + 1] = second.reshape(tiles_x, 8, 128)


def back_kernel(spectra, inverse_z, sample, search_to, search, sems):
    nx, ny, nz = sample.shape
    matrix = (inverse_z[0], inverse_z[1])
    copies = []
    for j in range(nx // 2):
        value = split(spectra[pl.ds(j, nz, stride=8)])
        smooth = dot_3(value, matrix, TRANSPOSED_LEFT)
        pair = slice(2 * j, 2 * j + 2)
        search[pair] = smooth.reshape(2, ny, nz) + sample[pair]
        copies.append(pltpu.make_async_copy(search.at[pair], search_to.at[pair], sems.at[j]))
        copies[-1].start()
    for copy in copies:
        copy.wait()


SMEM = pl.BlockSpec(memory_space=pltpu.SMEM)
VMEM = pl.BlockSpec(memory_space=pltpu.VMEM)
HBM = pl.BlockSpec(memory_space=pltpu.HBM)


def far(*sizes):
    return jax.ShapeDtypeStruct(sizes, F32)


def near(*sizes):
    return pltpu.VMEM(sizes, F32)


def call(kernel, scalars, stay, arrays, out_shape, out_specs, scratch, name):
    stay = [pltpu.with_memory_space_constraint(value, pltpu.HBM) for value in stay]
    arrays = [pltpu.with_memory_space_constraint(value, pltpu.VMEM) for value in arrays]
    return pl.pallas_call(
        kernel,
        out_shape=out_shape,
        in_specs=[SMEM] * len(scalars) + [HBM] * len(stay) + [VMEM] * len(arrays),
        out_specs=out_specs,
        scratch_shapes=scratch,
        compiler_params=pltpu.CompilerParams(vmem_limit_bytes=16 << 20),
        name=name,
    )(*scalars, *stay, *arrays)


def per_device(
    mean_field,
    log_scale,
    noise,
    wave_prev,
    wave_now,
    adjoint_next,
    adjoint_now,
    sources,
    receivers,
    observed,
    step_index,
    prior_scale,
):
    nx, ny, nz = wave_now.shape
    parts_x, parts_y = lax.axis_size("gx"), lax.axis_size("gy")
    total_x, total_y = nx * parts_x, ny * parts_y
    block = near(nx, ny, nz)
    flat = near(nx * ny, nz)

    sources, receivers = sources.T, receivers.T
    n_sources, n_receivers = sources.shape[1], receivers.shape[1]
    edge_x, edge_y = near(2, 4, ny, nz), near(2, nx // 2, 8, nz)
    xlow, xhigh, ylow, yhigh, field, speed, tilt, adjoint, sample, codes = call(
        edges_kernel,
        (),
        (sources, receivers, mean_field, log_scale, noise, adjoint_now, wave_now),
        (),
        (edge_x, edge_x, edge_y, edge_y, near(2, nx, ny + 16, nz), block, block, block, block)
        + (jax.ShapeDtypeStruct((1, n_sources + n_receivers), jnp.int32),),
        (VMEM,) * 10,
        [
            near(nx, ny, nz),
            near(nx, ny, nz),
            near(nx, ny, nz),
            pltpu.VMEM(sources.shape, jnp.int32),
            pltpu.VMEM(receivers.shape, jnp.int32),
            pltpu.SemaphoreType.DMA((3, 6)),
        ],
        "edges",
    )

    up_x = [(i, (i + 1) % parts_x) for i in range(parts_x)]
    down_x = [(j, i) for i, j in up_x]
    up_y = [(i, (i + 1) % parts_y) for i in range(parts_y)]
    down_y = [(j, i) for i, j in up_y]
    from_low_x = lax.ppermute(xhigh, "gx", up_x)
    from_high_x = lax.ppermute(xlow, "gx", down_x)
    from_low_y = lax.ppermute(yhigh, "gy", up_y)
    from_high_y = lax.ppermute(ylow, "gy", down_y)

    order = np.arange(total_x).reshape(parts_x, nx // 2, 2).transpose(2, 0, 1).reshape(-1)
    matrix_x = jnp.asarray(halves(hartley(total_x)[:, order]))
    matrix_y = jnp.asarray(halves(hartley(total_y)))
    terms_z = jnp.asarray(wave_terms(nz).astype(np.float32))
    bands = jnp.asarray(halves(band(nz)))
    curved, base_wave, base_adjoint, matrix_y, matrix_x, listed, counts, gains = call(
        local_kernel,
        (codes, prior_scale, terms_z),
        (wave_prev, adjoint_next, bands, matrix_y, matrix_x),
        (field, speed, adjoint),
        (block,) * 3
        + (
            pltpu.VMEM(matrix_y.shape, BF16),
            pltpu.VMEM(matrix_x.shape, BF16),
            jax.ShapeDtypeStruct((n_sources + n_receivers + 2,), jnp.int32),
            jax.ShapeDtypeStruct((n_receivers + 2,), jnp.int32),
            far(2),
        ),
        (VMEM,) * 5 + (SMEM,) * 3,
        [
            near(2, nx, ny, nz),
            near(nx, ny, nz),
            near(nx, ny, nz),
            pltpu.VMEM(bands.shape, BF16),
            pltpu.SemaphoreType.DMA((5,)),
        ],
        "local",
    )

    matrix_z = jnp.asarray(halves(hartley(nz)))
    wave_next, adjoint_prev, logscale_grad, spectra = call(
        finish_kernel,
        (codes, listed, counts, observed, step_index),
        (),
        (
            curved, base_wave, base_adjoint, speed, tilt,
            from_low_x, from_high_x, from_low_y, from_high_y, matrix_z,
        ),
        (pltpu.HBM((nx * ny, nz), F32),) * 3 + (far(nx * ny, nz),),
        (HBM,) * 3 + (VMEM,),
        [flat] * 4 + [pltpu.SemaphoreType.DMA((2 + nx // 2,))],
        "finish",
    )

    spectra = lax.all_to_all(
        spectra.reshape(nz, 8, nz), ("gx", "gy"), split_axis=0, concat_axis=0, tiled=True
    )

    terms_x = jnp.asarray(wave_terms(total_x).astype(np.float32)[:, None])
    terms_y = jnp.asarray(wave_terms(total_y).astype(np.float32)[None, :])
    filtered = call(
        filter_kernel,
        (gains,),
        (),
        (spectra.reshape(parts_x, parts_y, 8, nz), matrix_y, matrix_x, terms_x, terms_y),
        far(parts_x, parts_y, 8, nz),
        VMEM,
        [near(total_x, total_y)],
        "filter",
    )

    filtered = lax.all_to_all(
        filtered.reshape(nz, 8, nz), ("gx", "gy"), split_axis=0, concat_axis=0, tiled=True
    )
    search = call(
        back_kernel,
        (),
        (),
        (filtered.reshape(nx * ny, nz), matrix_z, sample),
        pltpu.HBM((nx, ny, nz), F32),
        HBM,
        [block, pltpu.SemaphoreType.DMA((nx // 2,))],
        "back",
    )
    return (
        wave_next.reshape(nx, ny, nz),
        adjoint_prev.reshape(nx, ny, nz),
        search,
        logscale_grad.reshape(nx, ny, nz),
    )


def solution(mesh):
    grid = P("gx", "gy", None)
    return jax.shard_map(
        per_device,
        mesh=mesh,
        in_specs=(grid,) * 7 + (P(),) * 5,
        out_specs=(grid,) * 4,
        check_vma=False,
    )
```

```python
import functools
import math

import jax
import jax.numpy as jnp
import numpy as np
from jax import lax
from jax.experimental import pallas as pl
from jax.experimental.pallas import tpu as pltpu
from jax.sharding import PartitionSpec as P

NSTEPS = 48
STENCIL_WEIGHTS = (-205.0 / 72.0, 8.0 / 5.0, -1.0 / 5.0, 8.0 / 315.0, -1.0 / 560.0)
COURANT_SQUARED = 0.08
VELOCITY_GAIN = 0.2
PULSE_FREQUENCY = 0.05
PULSE_AMPLITUDE = 20.0

F32 = jnp.float32
BF16 = jnp.bfloat16
ROW = (((1,), (0,)), ((), ()))
TRANSPOSED_RIGHT = (((1,), (1,)), ((), ()))
TRANSPOSED_LEFT = (((0,), (0,)), ((), ()))


def hartley(length):
    index = np.arange(length)
    angle = (index[:, None] * index[None, :] % length) * (2.0 * np.pi / length)
    return np.cos(angle) + np.sin(angle)


def halves(matrix):
    high = matrix.astype(np.float32).astype(jnp.bfloat16)
    low = (matrix - high.astype(np.float64)).astype(np.float32).astype(jnp.bfloat16)
    return np.stack([high, low])


def wave_terms(length):
    return (length / 8.0) ** 2 * 4.0 * np.sin(np.arange(length) * (np.pi / length)) ** 2


def band(length):
    matrix = np.zeros((length, length))
    for offset in range(5):
        weight = STENCIL_WEIGHTS[offset] * (3.0 if offset == 0 else 1.0)
        matrix += weight * np.eye(length, k=offset)
        if offset:
            matrix += weight * np.eye(length, k=-offset)
    return matrix


def split(value):
    high = value.astype(BF16)
    return high, (value - high.astype(F32)).astype(BF16)


def dot(left, right, dims=ROW):
    return lax.dot_general(left, right, dims, preferred_element_type=F32)


def dot_3(left, right, dims=ROW):
    (on_left,), (on_right,) = dims[0]
    if left[0].shape[on_left] <= 128:
        cross = dot(
            jnp.concatenate(left, axis=on_left), jnp.concatenate(right[::-1], axis=on_right), dims
        )
    else:
        cross = dot(left[0], right[1], dims) + dot(left[1], right[0], dims)
    return cross + dot(left[0], right[0], dims)


def edges_kernel(
    sources_from, receivers_from, mean_from, logs_from, noise_from, adjoint_from, wave_from,
    xlow, xhigh, ylow, yhigh, field, speed, tilt, adjoint, sample, codes,
    mean, logs, noise, sources, receivers, sems,
):
    nx, ny, nz = speed.shape
    n_sources, n_receivers = sources.shape[1], receivers.shape[1]
    rows = [slice(0, 4), slice(nx - 4, nx), slice(4, nx // 2), slice(nx // 2, nx - 4)]
    pairs = (
        (mean_from, mean),
        (logs_from, logs),
        (noise_from, noise),
        (adjoint_from, adjoint),
        (wave_from, field.at[0, :, 8 : ny + 8]),
    )
    copies = []
    for part in range(4):
        for i, (source, target) in enumerate(pairs):
            copy = pltpu.make_async_copy(
                source.at[rows[part]], target.at[rows[part]], sems.at[part, i]
            )
            copy.start()
            copies.append(copy)
    tables = [
        pltpu.make_async_copy(sources_from, sources, sems.at[0, 5]),
        pltpu.make_async_copy(receivers_from, receivers, sems.at[1, 5]),
    ]
    for copy in tables:
        copy.start()
    for kind in range(2):
        field[kind, :, 0:8] = jnp.zeros((nx, 8, nz), F32)
        field[kind, :, ny + 8 : ny + 16] = jnp.zeros((nx, 8, nz), F32)

    for part in range(4):
        for copy in copies[5 * part : 5 * part + 5]:
            copy.wait()
        for x in range(rows[part].start, rows[part].stop):
            spread_noise = jnp.exp(logs[x]) * noise[x]
            value = mean[x] + spread_noise
            sample[x] = value
            rate = COURANT_SQUARED * jnp.exp(2.0 * VELOCITY_GAIN * value)
            tilt[x] = spread_noise
            speed[x] = rate
            scaled = rate * adjoint[x]
            field[1, x, 8 : ny + 8] = scaled
            for kind in range(2):
                value = scaled if kind else field[0, x, 8 : ny + 8]
                if part == 0:
                    xlow[kind, x] = value
                elif part == 1:
                    xhigh[kind, x - nx + 4] = value
                half = slice(4 * (x % 2), 4 * (x % 2) + 4)
                ylow[kind, x // 2, half] = value[0:4]
                yhigh[kind, x // 2, half] = value[ny - 4 : ny]

    for copy in tables:
        copy.wait()

    def code(points):
        at_x = points[0:1] - lax.axis_index("gx") * nx
        at_y = points[1:2] - lax.axis_index("gy") * ny
        inside = (at_x >= 0) & (at_x < nx) & (at_y >= 0) & (at_y < ny)
        return jnp.where(inside, (at_x * ny + at_y) * nz + points[2:3], -1)

    codes[:, 0:n_receivers] = code(receivers)
    codes[:, n_receivers : n_receivers + n_sources] = code(sources)


def local_kernel(
    codes, prior_scale, terms_z, wave_prev_from, adjoint_next_from, bands_from, matrix_y_from, matrix_x_from,
    field, speed, adjoint,
    curved, base_wave, base_adjoint, matrix_y, matrix_x, listed, counts, gains,
    plane, wave_prev, adjoint_next, bands, sems,
):
    nx, ny, nz = speed.shape
    n_receivers = counts.shape[0] - 2
    n_sources = listed.shape[0] - 2 - n_receivers
    copies = [
        pltpu.make_async_copy(bands_from, bands, sems.at[0]),
        pltpu.make_async_copy(wave_prev_from, wave_prev, sems.at[1]),
        pltpu.make_async_copy(adjoint_next_from, adjoint_next, sems.at[2]),
        pltpu.make_async_copy(matrix_y_from, matrix_y, sems.at[3]),
        pltpu.make_async_copy(matrix_x_from, matrix_x, sems.at[4]),
    ]
    for copy in copies:
        copy.start()

    def scan(first, number, at, count):
        for i in range(number):
            listed[at + count] = first + i
            count = count + (codes[0, first + i] >= 0).astype(jnp.int32)
        return count

    copies[0].wait()
    pair = (bands[0], bands[1])
    for kind in range(2):
        for x in range(0, nx, 4):
            value = field[kind, x : x + 4, 8 : ny + 8].reshape(4 * ny, nz)
            plane[kind, x : x + 4] = dot_3(split(value), pair).reshape(4, ny, nz)
    for copy in copies[1:3]:
        copy.wait()

    def strip(t, count):
        start = pl.multiple_of(8 * t, 8)
        here = pl.ds(start, 8)
        for kind in range(2):
            centre = [field[kind, x, pl.ds(start + 8, 8)] for x in range(nx)]
            for x in range(nx):
                total = plane[kind, x, here]
                for offset in range(1, 5):
                    near_by = field[kind, x, pl.ds(start + 8 + offset, 8)]
                    near_by = near_by + field[kind, x, pl.ds(start + 8 - offset, 8)]
                    if x + offset < nx:
                        near_by = near_by + centre[x + offset]
                    if x - offset >= 0:
                        near_by = near_by + centre[x - offset]
                    total = total + STENCIL_WEIGHTS[offset] * near_by
                if kind == 0:
                    curved[x, here] = total
                    rest = 2.0 * centre[x] - wave_prev[x, here]
                    base_wave[x, here] = rest + speed[x, here] * total
                else:
                    rest = 2.0 * adjoint[x, here] - adjoint_next[x, here]
                    base_adjoint[x, here] = rest + total
        step = n_receivers // (ny // 8)
        some = scan(t * step, step, n_sources + 1, count[0])
        step = n_sources // (ny // 8)
        return some, scan(n_receivers + t * step, step, 0, count[1])

    found = lax.fori_loop(0, ny // 8, strip, (jnp.int32(0), jnp.int32(0)))
    counts[0], counts[1] = found[1], found[0]
    depth = lax.axis_index("gx") * lax.axis_size("gy") + lax.axis_index("gy")
    cells = matrix_x.shape[1] * matrix_y.shape[1] * nz
    gains[0] = prior_scale[0] * (math.sqrt(cells) / 8.0 / cells)
    gains[1] = 1.0 + terms_z[depth]
    for copy in copies[3:]:
        copy.wait()


def finish_kernel(
    codes, listed, counts, observed, step_index,
    curved, base_wave, base_adjoint, speed, tilt,
    xlow, xhigh, ylow, yhigh, forward_z,
    wave_to, adjoint_to, logscale_to, spectra,
    wave_next, adjoint_prev, logscale_grad, slope, sems,
):
    nx, ny, nz = curved.shape
    index_x, index_y = lax.axis_index("gx"), lax.axis_index("gy")
    n_receivers = counts.shape[0] - 2
    n_sources = listed.shape[0] - 2 - n_receivers
    row_at = lax.broadcasted_iota(jnp.int32, (8, nz), 0)
    lane_at = lax.broadcasted_iota(jnp.int32, (1, nz), 1)
    keep = [
        index_x > 0,
        index_x < lax.axis_size("gx") - 1,
        index_y > 0,
        index_y < lax.axis_size("gy") - 1,
    ]
    keep = [value.astype(F32) for value in keep]
    moment = jnp.full((1, nz), step_index[0] - NSTEPS // 2).astype(F32)
    moment = moment * (math.pi * PULSE_FREQUENCY)
    pulse = PULSE_AMPLITUDE * (1.0 - 2.0 * moment * moment) * jnp.exp(-moment * moment)

    def lateral_y(kind, x):
        start = jnp.zeros((8, nz), F32)
        end = jnp.zeros((8, nz), F32)
        low, high = ylow[kind, x // 2], yhigh[kind, x // 2]
        mine = row_at < 4 if x % 2 == 0 else row_at >= 4
        low, high = jnp.where(mine, low, 0.0), jnp.where(mine, high, 0.0)
        base = 0 if x % 2 == 0 else 4
        for offset in range(1, 5):
            start = start + STENCIL_WEIGHTS[offset] * pltpu.roll(low, (offset - 4 - base) % 8, 0)
            end = end + STENCIL_WEIGHTS[offset] * pltpu.roll(high, (8 - offset - base) % 8, 0)
        return jnp.where(row_at < 4, start, 0.0) * keep[2], jnp.where(row_at >= 4, end, 0.0) * keep[3]

    def change(kind, x, edges, first, last):
        total = None
        if first == 0:
            total = edges[0]
        elif last == ny:
            total = edges[1]
        for offset in range(1, 5):
            if x - offset < 0:
                layer, weight = xlow[kind, x - offset + 4, first:last], keep[0]
            elif x + offset >= nx:
                layer, weight = xhigh[kind, x + offset - nx, first:last], keep[1]
            else:
                continue
            term = STENCIL_WEIGHTS[offset] * weight * layer
            total = term if total is None else total + term
        return total

    for x in range(nx):
        edges = [lateral_y(kind, x) for kind in range(2)]
        for first, last in ((0, 8), (8, ny - 8), (ny - 8, ny)):
            rows = slice(x * ny + first, x * ny + last)
            bend, rate = curved[x, first:last], speed[x, first:last]
            onward, backward = base_wave[x, first:last], base_adjoint[x, first:last]
            more = change(0, x, edges[0], first, last)
            if more is not None:
                bend, onward = bend + more, onward + rate * more
                backward = backward + change(1, x, edges[1], first, last)
            wave_next[rows] = onward
            adjoint_prev[rows] = backward
            slope[rows] = (2.0 * VELOCITY_GAIN) * rate * bend

    def place(point):
        code = codes[0, point]
        return pl.ds(code // nz, 1), lane_at == code % nz

    def shoot(i, _):
        row, hit = place(listed[i])
        wave_next[row] = wave_next[row] + jnp.where(hit, pulse, 0.0)
        return 0

    lax.fori_loop(0, counts[0], shoot, 0)

    def record(i, _):
        point = listed[n_sources + 1 + i]
        row, hit = place(point)
        misfit = wave_next[row] - observed[point]
        adjoint_prev[row] = adjoint_prev[row] + jnp.where(hit, misfit, 0.0)
        return 0

    lax.fori_loop(0, counts[1], record, 0)

    copies = [
        pltpu.make_async_copy(wave_next, wave_to, sems.at[0]),
        pltpu.make_async_copy(adjoint_prev, adjoint_to, sems.at[1]),
    ]
    for copy in copies:
        copy.start()
    matrix = (forward_z[0], forward_z[1])
    for j in range(nx // 2):
        rows = slice(2 * j * ny, 2 * (j + 1) * ny)
        grad = slope[rows] * adjoint_prev[rows]
        logscale_grad[rows] = grad * tilt[2 * j : 2 * j + 2].reshape(2 * ny, nz) - 1.0
        spectra[pl.ds(j, nz, stride=8)] = dot_3(matrix, split(grad), TRANSPOSED_RIGHT)
        copy = pltpu.make_async_copy(logscale_grad.at[rows], logscale_to.at[rows], sems.at[2 + j])
        copy.start()
        copies.append(copy)
    for copy in copies:
        copy.wait()


def filter_kernel(gains, spectra, matrix_y, matrix_x, terms_x, terms_y, result, plane):
    half = plane.shape[0] // 2
    tiles_x, tiles_y = spectra.shape[0], spectra.shape[1]
    lane = lax.broadcasted_iota(jnp.int32, (half, 128), 1)
    for m in range(tiles_y // 2):
        even = spectra[:, 2 * m].reshape(half, 128)
        odd = spectra[:, 2 * m + 1].reshape(half, 128)
        columns = slice(128 * m, 128 * (m + 1))
        plane[0:half, columns] = jnp.where(lane < 64, even, pltpu.roll(odd, 64, 1))
        plane[half:, columns] = jnp.where(lane < 64, pltpu.roll(even, 64, 1), odd)
    pair_y = (matrix_y[0], matrix_y[1])
    pair_x = (matrix_x[0], matrix_x[1])
    value = dot_3(split(plane[...]), pair_y)
    value = dot_3(pair_x, split(value))
    value = value * (gains[0] / ((gains[1] + terms_x[...]) + terms_y[...]))
    value = dot_3(pair_x, split(value), TRANSPOSED_LEFT)
    plane[...] = dot_3(split(value), pair_y)
    for m in range(tiles_y // 2):
        columns = slice(128 * m, 128 * (m + 1))
        even, odd = plane[0:half, columns], plane[half:, columns]
        first = jnp.where(lane < 64, even, pltpu.roll(odd, 64, 1))
        second = jnp.where(lane < 64, pltpu.roll(even, 64, 1), odd)
        result[:, 2 * m] = first.reshape(tiles_x, 8, 128)
        result[:, 2 * m + 1] = second.reshape(tiles_x, 8, 128)


def back_kernel(spectra, inverse_z, sample, search_to, search, sems):
    nx, ny, nz = sample.shape
    matrix = (inverse_z[0], inverse_z[1])
    copies = []
    for j in range(nx // 2):
        value = split(spectra[pl.ds(j, nz, stride=8)])
        smooth = dot_3(value, matrix, TRANSPOSED_LEFT)
        pair = slice(2 * j, 2 * j + 2)
        search[pair] = smooth.reshape(2, ny, nz) + sample[pair]
        copies.append(pltpu.make_async_copy(search.at[pair], search_to.at[pair], sems.at[j]))
        copies[-1].start()
    for copy in copies:
        copy.wait()


SMEM = pl.BlockSpec(memory_space=pltpu.SMEM)
VMEM = pl.BlockSpec(memory_space=pltpu.VMEM)
HBM = pl.BlockSpec(memory_space=pltpu.HBM)


def far(*sizes):
    return jax.ShapeDtypeStruct(sizes, F32)


def near(*sizes):
    return pltpu.VMEM(sizes, F32)


def call(kernel, scalars, stay, arrays, out_shape, out_specs, scratch, name):
    stay = [pltpu.with_memory_space_constraint(value, pltpu.HBM) for value in stay]
    arrays = [pltpu.with_memory_space_constraint(value, pltpu.VMEM) for value in arrays]
    return pl.pallas_call(
        kernel,
        out_shape=out_shape,
        in_specs=[SMEM] * len(scalars) + [HBM] * len(stay) + [VMEM] * len(arrays),
        out_specs=out_specs,
        scratch_shapes=scratch,
        compiler_params=pltpu.CompilerParams(vmem_limit_bytes=16 << 20),
        name=name,
    )(*scalars, *stay, *arrays)


def per_device(
    mean_field,
    log_scale,
    noise,
    wave_prev,
    wave_now,
    adjoint_next,
    adjoint_now,
    sources,
    receivers,
    observed,
    step_index,
    prior_scale,
):
    nx, ny, nz = wave_now.shape
    parts_x, parts_y = lax.axis_size("gx"), lax.axis_size("gy")
    total_x, total_y = nx * parts_x, ny * parts_y
    block = near(nx, ny, nz)
    flat = near(nx * ny, nz)

    sources, receivers = sources.T, receivers.T
    n_sources, n_receivers = sources.shape[1], receivers.shape[1]
    edge_x, edge_y = near(2, 4, ny, nz), near(2, nx // 2, 8, nz)
    xlow, xhigh, ylow, yhigh, field, speed, tilt, adjoint, sample, codes = call(
        edges_kernel,
        (),
        (sources, receivers, mean_field, log_scale, noise, adjoint_now, wave_now),
        (),
        (edge_x, edge_x, edge_y, edge_y, near(2, nx, ny + 16, nz), block, block, block, block)
        + (jax.ShapeDtypeStruct((1, n_sources + n_receivers), jnp.int32),),
        (VMEM,) * 10,
        [
            near(nx, ny, nz),
            near(nx, ny, nz),
            near(nx, ny, nz),
            pltpu.VMEM(sources.shape, jnp.int32),
            pltpu.VMEM(receivers.shape, jnp.int32),
            pltpu.SemaphoreType.DMA((4, 6)),
        ],
        "edges",
    )

    up_x = [(i, (i + 1) % parts_x) for i in range(parts_x)]
    down_x = [(j, i) for i, j in up_x]
    up_y = [(i, (i + 1) % parts_y) for i in range(parts_y)]
    down_y = [(j, i) for i, j in up_y]
    from_low_x = lax.ppermute(xhigh, "gx", up_x)
    from_high_x = lax.ppermute(xlow, "gx", down_x)
    from_low_y = lax.ppermute(yhigh, "gy", up_y)
    from_high_y = lax.ppermute(ylow, "gy", down_y)

    order = np.arange(total_x).reshape(parts_x, nx // 2, 2).transpose(2, 0, 1).reshape(-1)
    matrix_x = jnp.asarray(halves(hartley(total_x)[:, order]))
    matrix_y = jnp.asarray(halves(hartley(total_y)))
    terms_z = jnp.asarray(wave_terms(nz).astype(np.float32))
    bands = jnp.asarray(halves(band(nz)))
    curved, base_wave, base_adjoint, matrix_y, matrix_x, listed, counts, gains = call(
        local_kernel,
        (codes, prior_scale, terms_z),
        (wave_prev, adjoint_next, bands, matrix_y, matrix_x),
        (field, speed, adjoint),
        (block,) * 3
        + (
            pltpu.VMEM(matrix_y.shape, BF16),
            pltpu.VMEM(matrix_x.shape, BF16),
            jax.ShapeDtypeStruct((n_sources + n_receivers + 2,), jnp.int32),
            jax.ShapeDtypeStruct((n_receivers + 2,), jnp.int32),
            far(2),
        ),
        (VMEM,) * 5 + (SMEM,) * 3,
        [
            near(2, nx, ny, nz),
            near(nx, ny, nz),
            near(nx, ny, nz),
            pltpu.VMEM(bands.shape, BF16),
            pltpu.SemaphoreType.DMA((5,)),
        ],
        "local",
    )

    matrix_z = jnp.asarray(halves(hartley(nz)))
    wave_next, adjoint_prev, logscale_grad, spectra = call(
        finish_kernel,
        (codes, listed, counts, observed, step_index),
        (),
        (
            curved, base_wave, base_adjoint, speed, tilt,
            from_low_x, from_high_x, from_low_y, from_high_y, matrix_z,
        ),
        (pltpu.HBM((nx * ny, nz), F32),) * 3 + (far(nx * ny, nz),),
        (HBM,) * 3 + (VMEM,),
        [flat] * 4 + [pltpu.SemaphoreType.DMA((2 + nx // 2,))],
        "finish",
    )

    spectra = lax.all_to_all(
        spectra.reshape(nz, 8, nz), ("gx", "gy"), split_axis=0, concat_axis=0, tiled=True
    )

    terms_x = jnp.asarray(wave_terms(total_x).astype(np.float32)[:, None])
    terms_y = jnp.asarray(wave_terms(total_y).astype(np.float32)[None, :])
    filtered = call(
        filter_kernel,
        (gains,),
        (),
        (spectra.reshape(parts_x, parts_y, 8, nz), matrix_y, matrix_x, terms_x, terms_y),
        far(parts_x, parts_y, 8, nz),
        VMEM,
        [near(total_x, total_y)],
        "filter",
    )

    filtered = lax.all_to_all(
        filtered.reshape(nz, 8, nz), ("gx", "gy"), split_axis=0, concat_axis=0, tiled=True
    )
    search = call(
        back_kernel,
        (),
        (),
        (filtered.reshape(nx * ny, nz), matrix_z, sample),
        pltpu.HBM((nx, ny, nz), F32),
        HBM,
        [block, pltpu.SemaphoreType.DMA((nx // 2,))],
        "back",
    )
    return (
        wave_next.reshape(nx, ny, nz),
        adjoint_prev.reshape(nx, ny, nz),
        search,
        logscale_grad.reshape(nx, ny, nz),
    )


def solution(mesh):
    grid = P("gx", "gy", None)
    return jax.shard_map(
        per_device,
        mesh=mesh,
        in_specs=(grid,) * 7 + (P(),) * 5,
        out_specs=(grid,) * 4,
        check_vma=False,
    )
```
